128 devices in a mesh: xline: 16 (over z, x), iline: 8 (over y, core).
Axes of the slice: x: 4, y: 4, z: 4, core: 2. Of those that a mesh axis runs over, the one named last changes fastest.
Arguments:
- traces: bfloat16 [65536, 1536], P(('xline', 'iline')), may hold values from -16 to 16
- trace_offset: bfloat16 [65536], P(('xline', 'iline')), may hold values from 0 to 1
- trace_owner: int32 [65536], P(('xline', 'iline')), may hold values from 0 to 127, as said below
- trace_cell: int32 [65536], P(('xline', 'iline')), may hold values from 0 to 7
- slowness: float32 [32, 32, 1536], P('xline', 'iline'), may hold values from 1 to 36
- band_start: int32 [1536], replicated, may hold values from 0 to 1528, as said below
- dip_shift: int32 [9, 32, 32], P(None, 'xline', 'iline'), may hold values from -4 to 4
Outputs:
- smoothed: float32 [32, 32, 1536], P('xline', 'iline')
The draws below stay inside these ranges and needn't reach their ends.
Inputs may be any that keep to these rules, and one draw needn't show every extreme that they name: `trace_owner`: at most 5 traces of one device (one aligned block of 512 rows) share a bin block, and one particular bin block receives exactly 5 traces from every device. band_start[t] - t lies between -(7) and 0 for every t.
All inputs are finite; a program needn't handle non-finite values.
Results may differ from the reference program's by a relative error of at most 0.0003.
Values may be sent and summed in bfloat16 or wider, within the bound.
No kernel may reach another device: no remote copies, remote signals or barrier semaphores. Data moves between devices by JAX's collectives and lax.ppermute only.
A program may use at most 64 MiB of HBM per device.

```python
import math
import jax
import jax.numpy as jnp
from jax import lax

NT = 1536
BAND = 8
DIP = 4
TR_DEV = 512
BX = 2
BY = 4
OWNERS = 128
TRACES = 65536
NBX = 32
NBY = 32
BIN_DEV = 8
CAP = 5
N_ILINE = 8


def owner_table(key):
    base_key = jax.random.fold_in(key, 7)
    key_hot, key_popular, key_rest = jax.random.split(base_key, 3)
    hot_owner = jax.random.randint(key_hot, (), 0, OWNERS).astype(jnp.int32)
    popularity = jax.random.randint(key_popular, (OWNERS,), 0, 4) * (1 << 18)
    slot_owner = jnp.arange(OWNERS * CAP, dtype=jnp.int32) // CAP

    def one_block(block_id):
        block_key = jax.random.fold_in(key_rest, block_id)
        key_score, key_order = jax.random.split(block_key)
        scores = jax.random.randint(key_score, (OWNERS * CAP,), 0, 1 << 20) + popularity[slot_owner]
        scores = jnp.where(slot_owner == hot_owner, -1, scores)
        ranked = jnp.argsort(-scores, stable=True)
        picked = slot_owner[ranked[:TR_DEV - CAP]]
        chosen = jnp.concatenate([jnp.full((CAP,), hot_owner, jnp.int32), picked.astype(jnp.int32)])
        return jax.random.permutation(key_order, chosen)
    return jax.vmap(one_block)(jnp.arange(OWNERS)).reshape(TRACES).astype(jnp.int32)


def draw_trace_owner(key, part):
    return owner_table(key)


def draw_trace_cell(key, part):
    owner_rows = owner_table(key)
    cell_key = jax.random.fold_in(key, 11)
    key_cell, key_hole = jax.random.split(cell_key)
    cell_draw = jax.random.randint(key_cell, (TRACES,), 0, BIN_DEV)
    hole_index = jax.random.randint(key_hole, (OWNERS,), 0, 2 * BIN_DEV)
    hole_rows = hole_index[owner_rows]
    return jnp.where(cell_draw == hole_rows, (cell_draw + 1) % BIN_DEV, cell_draw).astype(jnp.int32)


def draw_band_start(key, part):
    spread = jax.random.randint(jax.random.fold_in(key, 13), (NT,), 0, BAND)
    band_begin = jnp.arange(NT, dtype=jnp.int32) + spread - BAND + 1
    return jnp.clip(band_begin, 0, NT - BAND).astype(jnp.int32)


def plant(values, stream_key, smallest, top_value):
    extent = values.shape
    index_at = [jax.random.randint(jax.random.fold_in(stream_key, axis), (), 0, extent[axis]) for axis in range(len(extent))]
    values = values.at[tuple(index_at)].set(smallest)
    longest = extent.index(max(extent))
    index_at[longest] = (index_at[longest] + 1) % extent[longest]
    return values.at[tuple(index_at)].set(top_value)


def shard_levels(own_key, extent, cuts, least, high):
    gain, own = 1.0, jax.random.fold_in(own_key, 6)
    for dim, blocks in cuts:
        steps = jnp.exp(jax.random.uniform(jax.random.fold_in(own, dim), (blocks,), jnp.float32, least / len(cuts), high / len(cuts)))
        gain = gain * jnp.repeat(steps, extent[dim] // blocks).reshape([-1 if axis == dim else 1 for axis in range(len(extent))])
    return gain


def gaussian(key, shape, scale, bound, cuts=(), kind=jnp.bfloat16):
    loudness = shard_levels(key, shape, cuts, -0.22, 0.18) if cuts else 1.0
    values = jax.random.normal(key, shape, jnp.float32) * scale * loudness
    return jnp.minimum(jnp.maximum(values, -bound), bound).astype(kind)


def setup_inputs(seed: int = 0) -> dict:
    key_list = jax.random.split(jax.random.key(seed), 8)
    return {
        "traces": gaussian(key_list[0], (TRACES, NT), 4.0, 16.0, ((0, 128),)),
        "trace_offset": jnp.clip(1.0 * jax.random.uniform(key_list[1], (TRACES,), jnp.float32) ** shard_levels(key_list[1], (TRACES,), ((0, 128),), -0.2, 0.2), 0.0, 1.0).astype(jnp.bfloat16),
        "trace_owner": draw_trace_owner(jax.random.fold_in(key_list[7], 71), 0),
        "trace_cell": draw_trace_cell(jax.random.fold_in(key_list[7], 71), 0),
        "slowness": jnp.clip(jnp.exp(math.log(36.0) - 3.583519 * jax.random.uniform(key_list[4], (NBX, NBY, NT), jnp.float32) ** shard_levels(key_list[4], (NBX, NBY, NT), ((0, 16), (1, 8)), -0.2, 0.2)), 1.0, 36.0),
        "band_start": draw_band_start(jax.random.fold_in(key_list[7], 71), 0),
        "dip_shift": plant(jax.random.randint(key_list[6], (9, NBX, NBY), -DIP, DIP + 1), jax.random.fold_in(key_list[6], 1), -DIP, DIP).astype(jnp.int32),
    }


CENTER_WEIGHT = 0.5
SIDE_WEIGHT = 0.0625

def corrected_rows(trace_rows, offset_rows, slow_rows, band_start):
    samples = trace_rows.shape[1]
    sample_times = jnp.arange(samples).astype(jnp.float32)
    moveout = jnp.sqrt(sample_times[None, :] * sample_times[None, :] + (offset_rows * offset_rows)[:, None] * slow_rows)
    numerator = jnp.zeros(moveout.shape, jnp.float32)
    denominator = jnp.zeros(moveout.shape, jnp.float32)
    for band_lag in range(BAND):
        position = band_start + band_lag
        picked = jnp.take(trace_rows, position, axis=1).astype(jnp.float32)
        distance = position.astype(jnp.float32)[None, :] - moveout
        weight = 1.0 / (1.0 + distance * distance)
        numerator = numerator + weight * picked
        denominator = denominator + weight
    return numerator / denominator

def smooth_bins(padded, dip_shift, rows_x, rows_y):
    samples = padded.shape[2]
    sample_times = jnp.arange(samples, dtype=jnp.int32)
    result = jnp.zeros((rows_x, rows_y, samples), jnp.float32)
    for neighbour in range(9):
        shift_x = neighbour // 3
        shift_y = neighbour % 3
        window = padded[shift_x:shift_x + rows_x, shift_y:shift_y + rows_y, :]
        widened = jnp.pad(window, ((0, 0), (0, 0), (DIP, DIP)))
        position = sample_times[None, None, :] + dip_shift[neighbour][:, :, None] + DIP
        shifted = jnp.take_along_axis(widened, position.astype(jnp.int32), axis=2)
        factor = CENTER_WEIGHT if neighbour == 4 else SIDE_WEIGHT
        result = result + factor * shifted
    return result

def reference(traces, trace_offset, trace_owner, trace_cell, slowness, band_start, dip_shift):
    bin_x = trace_owner // N_ILINE * BX + trace_cell // BY
    bin_y = trace_owner % N_ILINE * BY + trace_cell % BY
    bin_of = (bin_x * NBY + bin_y).astype(jnp.int32)
    slow_table = slowness.reshape(NBX * NBY, NT)

    def accumulate(running, block_parts):
        block_traces, block_offsets, block_bins = block_parts
        slow_rows = slow_table[block_bins]
        moved = corrected_rows(block_traces, block_offsets.astype(jnp.float32), slow_rows, band_start)
        return (running.at[block_bins].add(moved), None)
    blocks = (traces.reshape(OWNERS, TR_DEV, NT), trace_offset.reshape(OWNERS, TR_DEV), bin_of.reshape(OWNERS, TR_DEV))
    bin_sums, unused = lax.scan(accumulate, jnp.zeros((NBX * NBY, NT), jnp.float32), blocks)
    fold_count = jnp.zeros((NBX * NBY,), jnp.int32).at[bin_of].add(1)
    bin_stack = (bin_sums / jnp.maximum(fold_count, 1).astype(jnp.float32)[:, None]).reshape(NBX, NBY, NT)
    padded = jnp.pad(bin_stack, ((1, 1), (1, 1), (0, 0)))
    return smooth_bins(padded, dip_shift, NBX, NBY)
```

```python
import functools

import jax
import jax.numpy as jnp
from jax import lax
from jax.experimental import pallas as pl
from jax.experimental.pallas import tpu as pltpu
from jax.sharding import PartitionSpec as P

BAND = 8
DIP = 4
REACH = BAND - 1
LANES = 128
CAP = 5
ROWS = 64
HALVES = (0.5, 1.5, 2.5, 3.5)

CENTER_WEIGHT = 0.5
SIDE_WEIGHT = 0.0625

AXES = ("xline", "iline")
F32 = jnp.float32
BF16 = jnp.bfloat16


def iota(shape, dim):
    return lax.broadcasted_iota(jnp.int32, shape, dim)


def dispatch_kernel(owners, traces_ref, owner_ref, cell_ref, offset_ref, out_ref, stage):
    rows, samples = traces_ref.shape
    blocks = samples // LANES
    owner = owner_ref[...]
    is_owner = iota((owners, rows), 0) == owner
    hot = is_owner.astype(F32)
    earlier = (iota((rows, rows), 0) < iota((rows, rows), 1)).astype(F32).astype(BF16)
    counts = jnp.dot(hot.astype(BF16), earlier, preferred_element_type=F32)
    rank = jnp.sum(hot * counts, axis=0, keepdims=True)
    picks = [jnp.where(rank == float(k), hot, 0.0).astype(BF16) for k in range(CAP)]
    pick = jnp.concatenate(picks, axis=0)
    meta = jnp.zeros((owners, LANES), F32)
    line = iota((LANES, rows), 0)
    offset = offset_ref[...]
    cell = (cell_ref[...] + 1).astype(F32)
    for k in range(CAP):
        source = jnp.where(line == 8 * k, offset, jnp.where(line == 8 * k + 1, cell, 0.0))
        meta = meta + lax.dot_general(
            picks[k], source.astype(BF16), (((1,), (1,)), ((), ())), preferred_element_type=F32
        )
    stage[pl.ds(CAP * blocks, owners, stride=ROWS), :] = meta
    for row in range(CAP * blocks + 1, ROWS):
        stage[pl.ds(row, owners, stride=ROWS), :] = jnp.zeros((owners, LANES), F32)
    placed = jnp.dot(pick, traces_ref[...], preferred_element_type=F32)
    placed = pltpu.roll(placed, REACH, 1)
    for k in range(CAP):
        for block in range(blocks):
            stage[pl.ds(k * blocks + block, owners, stride=ROWS), :] = placed[
                k * owners : (k + 1) * owners, block * LANES : (block + 1) * LANES
            ]
    out_ref[...] = stage[...].astype(BF16)


def dispatch(traces, owner, cell, offset, owners):
    rows, samples = traces.shape
    return pl.pallas_call(
        functools.partial(dispatch_kernel, owners),
        out_shape=jax.ShapeDtypeStruct((owners * ROWS, LANES), BF16),
        scratch_shapes=[pltpu.VMEM((owners * ROWS, LANES), F32)],
        name="dispatch",
    )(traces, owner.reshape(1, rows), cell.reshape(1, rows), offset.astype(F32).reshape(1, rows))


def bands_kernel(start_ref, out_ref):
    block = pl.program_id(0)
    first = start_ref[...] + (REACH - block * LANES)
    place = iota((2 * LANES, LANES), 0) - first
    for i, half in enumerate(HALVES):
        low = (place == int(3.5 - half)).astype(F32)
        high = (place == int(3.5 + half)).astype(F32)
        out_ref[0, :, i * LANES : (i + 1) * LANES] = (0.5 * (low + high)).astype(BF16)
        out_ref[0, :, (4 + i) * LANES : (5 + i) * LANES] = (half * (low - high)).astype(BF16)


def bands(band_start):
    samples = band_start.shape[0]
    blocks = samples // LANES
    return pl.pallas_call(
        bands_kernel,
        grid=(blocks,),
        in_specs=[pl.BlockSpec((1, LANES), lambda b: (0, b))],
        out_specs=pl.BlockSpec((1, 2 * LANES, BAND * LANES), lambda b: (b, 0, 0)),
        out_shape=jax.ShapeDtypeStruct((blocks, 2 * LANES, BAND * LANES), BF16),
        name="bands",
    )(band_start.reshape(1, samples))


def split3(value):
    high = value.astype(BF16)
    rest = value - high.astype(F32)
    middle = rest.astype(BF16)
    low = (rest - middle.astype(F32)).astype(BF16)
    return high, middle, low


def correct(lag, pairs):
    square = lag * lag
    fourth = square * square
    near = [square + (1.0 + h * h) for h in HALVES]
    prod = [(fourth + (1.0 + h * h) ** 2) + (2.0 - 2.0 * h * h) * square for h in HALVES]
    top = [pairs[i] * near[i] + pairs[4 + i] * lag for i in range(4)]
    left, right = prod[0] * prod[1], prod[2] * prod[3]
    num = (top[0] * prod[1] + top[1] * prod[0]) * right + (top[2] * prod[3] + top[3] * prod[2]) * left
    den = (near[0] * prod[1] + near[1] * prod[0]) * right + (near[2] * prod[3] + near[3] * prod[2]) * left
    return num / den


def stack_kernel(got_ref, bands_ref, start_ref, slow_ref, out_ref, stage, window, scaled, member, fold, pairs, moved):
    block = pl.program_id(0)
    blocks = pl.num_programs(0)
    bins = slow_ref.shape[0]
    sources = got_ref.shape[0] // ROWS
    items = CAP * sources

    @pl.when(block == 0)
    def _():
        stage[...] = got_ref[...].astype(F32)
        for k in range(CAP):
            for b in range(window.shape[0] - 1):
                rows = stage[pl.ds(k * (window.shape[0] - 1) + b, sources, stride=ROWS), :].astype(BF16)
                window[b, k * sources : (k + 1) * sources, :] = rows
                if b == 0:
                    window[window.shape[0] - 1, k * sources : (k + 1) * sources, :] = rows
        meta = stage[pl.ds(CAP * (window.shape[0] - 1), sources, stride=ROWS), :]
        across = meta.T
        lane = iota((sources, LANES), 1)
        total = jnp.zeros((bins, 1), F32)
        for k in range(CAP):
            offset = meta[:, 8 * k : 8 * k + 1]
            cell = meta[:, 8 * k + 1 : 8 * k + 2] - 1.0
            square = offset * offset
            high = square.astype(BF16).astype(F32)
            low = square - high
            part = jnp.where(lane < 3 * bins, high, low)
            keep = ((lane % bins).astype(F32) == cell) & (lane < 6 * bins)
            scaled[k * sources : (k + 1) * sources, :] = jnp.where(keep, part, 0.0).astype(BF16)
            same = across[8 * k + 1 : 8 * k + 2, :] == (iota((bins, sources), 0) + 1).astype(F32)
            ones = same.astype(F32)
            total = total + jnp.sum(ones, axis=1, keepdims=True)
            member[:, k * sources : (k + 1) * sources] = ones.astype(BF16)
        fold[...] = jnp.broadcast_to(jnp.maximum(total, 1.0), fold.shape)

    wide = jnp.concatenate([window[block], window[block + 1]], axis=1)
    pairs[...] = jnp.dot(wide, bands_ref[0], preferred_element_type=F32)
    parts = list(split3(slow_ref[...]))
    table = jnp.concatenate([p.astype(F32) for p in parts + parts] + [jnp.zeros((LANES - 6 * bins, LANES), F32)], axis=0)
    added = jnp.dot(scaled[...], table.astype(BF16), preferred_element_type=F32)
    time = (iota((1, LANES), 1) + block * LANES).astype(F32)
    start = start_ref[...].astype(F32) + 3.5
    step = 32
    for row in range(0, items, step):
        here = slice(row, row + step)
        lag = start - jnp.sqrt(time * time + added[here, :])
        got = [pairs[here, i * LANES : (i + 1) * LANES] for i in range(BAND)]
        value = correct(lag, got)
        high = value.astype(BF16)
        moved[here, :] = high
        moved[items + row : items + row + step, :] = (value - high.astype(F32)).astype(BF16)
    sums = jnp.dot(member[...], moved[:items, :], preferred_element_type=F32) + jnp.dot(
        member[...], moved[items:, :], preferred_element_type=F32
    )
    out_ref[...] = sums / fold[...]


def stack(got, picks, band_start, slowness):
    bins, samples = slowness.shape
    blocks = samples // LANES
    sources = got.shape[0] // ROWS
    items = CAP * sources
    return pl.pallas_call(
        stack_kernel,
        grid=(blocks,),
        in_specs=[
            pl.BlockSpec(got.shape, lambda b: (0, 0)),
            pl.BlockSpec((1, 2 * LANES, BAND * LANES), lambda b: (b, 0, 0)),
            pl.BlockSpec((1, LANES), lambda b: (0, b)),
            pl.BlockSpec((bins, LANES), lambda b: (0, b)),
        ],
        out_specs=pl.BlockSpec((bins, LANES), lambda b: (0, b)),
        out_shape=jax.ShapeDtypeStruct((bins, samples), F32),
        scratch_shapes=[
            pltpu.VMEM(got.shape, F32),
            pltpu.VMEM((blocks + 1, items, LANES), BF16),
            pltpu.VMEM((items, LANES), BF16),
            pltpu.VMEM((bins, items), BF16),
            pltpu.VMEM((bins, LANES), F32),
            pltpu.VMEM((items, BAND * LANES), F32),
            pltpu.VMEM((2 * items, LANES), BF16),
        ],
        name="stack",
    )(got, picks, band_start.reshape(1, samples), slowness)


def smooth_kernel(rows_x, rows_y, padded_ref, dip_ref, out_ref):
    bins = rows_x * rows_y
    samples = padded_ref.shape[2]
    near = []
    for n in range(9):
        dx, dy = n // 3, n % 3
        near.append(
            jnp.concatenate([padded_ref[dx + x, dy : dy + rows_y, :] for x in range(rows_x)], axis=0)
        )
    time = iota((bins, samples), 1)
    result = jnp.zeros((bins, samples), F32)
    for lag in range(-DIP, DIP + 1):
        part = jnp.zeros((bins, samples), F32)
        for n in range(9):
            factor = CENTER_WEIGHT if n == 4 else SIDE_WEIGHT
            weight = jnp.where(dip_ref[:, n : n + 1] == lag, factor, 0.0)
            part = part + weight * near[n]
        if lag:
            part = pltpu.roll(part, (-lag) % samples, 1)
            part = jnp.where((time + lag >= 0) & (time + lag < samples), part, 0.0)
        result = result + part
    out_ref[...] = result


def smooth(padded, dip, rows_x, rows_y):
    samples = padded.shape[2]
    return pl.pallas_call(
        functools.partial(smooth_kernel, rows_x, rows_y),
        out_shape=jax.ShapeDtypeStruct((rows_x * rows_y, samples), F32),
        name="smooth",
    )(padded, dip)


def with_halo(value, sides, width):
    for axis, dim in sides:
        size, length = (lax.axis_size(axis), value.shape[dim])
        up = [(i, (i + 1) % size) for i in range(size - 1)]
        down = [(j, i) for i, j in up]
        last = lax.slice_in_dim(value, length - width, length, axis=dim)
        initial = lax.slice_in_dim(value, 0, width, axis=dim)
        before = lax.ppermute(last, axis, up)
        after = lax.ppermute(initial, axis, down)
        value = jnp.concatenate([before, value, after], axis=dim)
    return value


def body(traces, trace_offset, trace_owner, trace_cell, slowness, band_start, dip_shift):
    owners = lax.axis_size(AXES)
    rows_x, rows_y, samples = slowness.shape
    bins = rows_x * rows_y
    send = dispatch(traces, trace_owner, trace_cell, trace_offset, owners)
    got = lax.all_to_all(send.reshape(owners, ROWS, LANES), AXES, split_axis=0, concat_axis=0, tiled=True)
    picks = bands(band_start)
    stacked = stack(got.reshape(owners * ROWS, LANES), picks, band_start, slowness.reshape(bins, samples))
    padded = with_halo(stacked.reshape(rows_x, rows_y, samples), (("xline", 0), ("iline", 1)), 1)
    dip = jnp.pad(dip_shift.reshape(9, bins).T, ((0, 0), (0, LANES - 9)))
    return smooth(padded, dip, rows_x, rows_y).reshape(rows_x, rows_y, samples)


def solution(mesh):
    return jax.shard_map(
        body,
        mesh=mesh,
        in_specs=(
            P(AXES, None),
            P(AXES),
            P(AXES),
            P(AXES),
            P("xline", "iline", None),
            P(),
            P(None, "xline", "iline"),
        ),
        out_specs=P("xline", "iline", None),
        check_vma=False,
    )
```

```python
import functools

import jax
import jax.numpy as jnp
from jax import lax
from jax.experimental import pallas as pl
from jax.experimental.pallas import tpu as pltpu
from jax.sharding import PartitionSpec as P

BAND = 8
DIP = 4
REACH = BAND - 1
LANES = 128
CAP = 5
ROWS = 64
PITCH = 65
STEP = 32
HALVES = (0.5, 1.5, 2.5, 3.5)
VMEM = pl.BlockSpec(memory_space=pltpu.VMEM)

CENTER_WEIGHT = 0.5
SIDE_WEIGHT = 0.0625

AXES = ("xline", "iline")
F32 = jnp.float32
BF16 = jnp.bfloat16


def iota(shape, dim):
    return lax.broadcasted_iota(jnp.int32, shape, dim)


def dispatch_kernel(owners, traces_hbm, owner_ref, cell_ref, offset_ref, out_ref, traces_ref, stage, arrived):
    copy = pltpu.make_async_copy(traces_hbm, traces_ref, arrived)
    copy.start()
    rows, samples = traces_ref.shape
    blocks = samples // LANES
    owner = owner_ref[...]
    hot = (iota((owners, rows), 0) == owner).astype(F32)
    earlier = (iota((rows, rows), 0) < iota((rows, rows), 1)).astype(F32).astype(BF16)
    counts = jnp.dot(hot.astype(BF16), earlier, preferred_element_type=F32)
    rank = jnp.sum(hot * counts, axis=0, keepdims=True)
    picks = [jnp.where(rank == float(k), hot, 0.0).astype(BF16) for k in range(CAP)]
    pick = jnp.concatenate(picks, axis=0)
    meta = jnp.zeros((owners, LANES), F32)
    line = iota((LANES, rows), 0)
    offset = offset_ref[...]
    cell = (cell_ref[...] + 1).astype(F32)
    for k in range(CAP):
        source = jnp.where(line == 8 * k, offset, jnp.where(line == 8 * k + 1, cell, 0.0))
        meta = meta + lax.dot_general(
            picks[k], source.astype(BF16), (((1,), (1,)), ((), ())), preferred_element_type=F32
        )
    stage[pl.ds(CAP * blocks, owners, stride=PITCH), :] = meta
    for row in range(CAP * blocks + 1, ROWS):
        stage[pl.ds(row, owners, stride=PITCH), :] = jnp.zeros((owners, LANES), F32)
    copy.wait()
    wrapped = iota((CAP * owners, LANES), 1) < REACH

    def put(block, value):
        for k in range(CAP):
            stage[pl.ds(k * blocks + block, owners, stride=PITCH), :] = value[k * owners : (k + 1) * owners, :]

    first = previous = None
    for tile in range(0, samples, 2 * LANES):
        placed = jnp.dot(pick, traces_ref[:, tile : tile + 2 * LANES], preferred_element_type=F32)
        for half in range(2):
            turned = pltpu.roll(placed[:, half * LANES : (half + 1) * LANES], REACH, 1)
            if first is None:
                first = turned
            else:
                put(tile // LANES + half, jnp.where(wrapped, previous, turned))
            previous = turned
    put(0, jnp.where(wrapped, previous, first))
    for owner_row in range(owners):
        out_ref[owner_row * ROWS : (owner_row + 1) * ROWS, :] = stage[
            owner_row * PITCH : owner_row * PITCH + ROWS, :
        ].astype(BF16)


def dispatch(traces, owner, cell, offset, owners):
    rows, samples = traces.shape
    return pl.pallas_call(
        functools.partial(dispatch_kernel, owners),
        in_specs=[pl.BlockSpec(memory_space=pl.ANY), VMEM, VMEM, VMEM],
        out_specs=VMEM,
        out_shape=jax.ShapeDtypeStruct((owners * ROWS, LANES), BF16),
        scratch_shapes=[
            pltpu.VMEM((rows, samples), BF16),
            pltpu.VMEM((owners * PITCH, LANES), F32),
            pltpu.SemaphoreType.DMA,
        ],
        compiler_params=pltpu.CompilerParams(vmem_limit_bytes=24 << 20),
        name="dispatch",
    )(traces, owner.reshape(1, rows), cell.reshape(1, rows), offset.astype(F32).reshape(1, rows))


def bands_kernel(start_ref, out_ref):
    for block in range(out_ref.shape[0]):
        first = start_ref[:, block * LANES : (block + 1) * LANES] + (REACH - block * LANES)
        place = iota((2 * LANES, LANES), 0) - first
        for lag in range(BAND):
            out_ref[block, :, lag * LANES : (lag + 1) * LANES] = (place == lag).astype(F32).astype(BF16)


def bands(band_start):
    samples = band_start.shape[0]
    blocks = samples // LANES
    return pl.pallas_call(
        bands_kernel,
        in_specs=[VMEM],
        out_specs=VMEM,
        out_shape=jax.ShapeDtypeStruct((blocks, 2 * LANES, BAND * LANES), BF16),
        compiler_params=pltpu.CompilerParams(vmem_limit_bytes=24 << 20),
        name="bands",
    )(band_start.reshape(1, samples))


def split3(value):
    high = value.astype(BF16)
    rest = value - high.astype(F32)
    middle = rest.astype(BF16)
    low = (rest - middle.astype(F32)).astype(BF16)
    return high, middle, low


def correct(lag, band):
    square = lag * lag
    num = den = None
    for i, half in enumerate(HALVES):
        even, odd = square + (1.0 + half * half), lag * (2.0 * half)
        low, high = 1.0 / (even - odd), 1.0 / (even + odd)
        below, above = int(3.5 - half), int(3.5 + half)
        part = band(below) * low + band(above) * high
        both = low + high
        num, den = (part, both) if num is None else (num + part, den + both)
    return num / den


def stack_kernel(got_ref, bands_ref, start_ref, slow_ref, out_ref, first_ref, last_ref, stage, window, scaled, member, fold, pairs0, pairs1, added0, added1, moved0, moved1):
    blocks = bands_ref.shape[0]
    bins = slow_ref.shape[0]
    sources = got_ref.shape[0] // ROWS
    items = CAP * sources
    for src in range(sources):
        stage[src * PITCH : src * PITCH + ROWS, :] = got_ref[src * ROWS : (src + 1) * ROWS, :].astype(F32)
    meta = stage[pl.ds(CAP * blocks, sources, stride=PITCH), :]
    across = meta.T
    lane = iota((sources, LANES), 1)
    total = jnp.zeros((bins, 1), F32)
    for k in range(CAP):
        here = slice(k * sources, (k + 1) * sources)
        for b in range(blocks):
            rows = stage[pl.ds(k * blocks + b, sources, stride=PITCH), :].astype(BF16)
            window[b, here, :] = rows
            if b == 0:
                window[blocks, here, :] = rows
        offset = meta[:, 8 * k : 8 * k + 1]
        cell = meta[:, 8 * k + 1 : 8 * k + 2] - 1.0
        square = offset * offset
        high = square.astype(BF16).astype(F32)
        part = jnp.where(lane < 3 * bins, high, square - high)
        keep = ((lane % bins).astype(F32) == cell) & (lane < 6 * bins)
        scaled[here, :] = jnp.where(keep, part, 0.0).astype(BF16)
        ones = (across[8 * k + 1 : 8 * k + 2, :] == (iota((bins, sources), 0) + 1).astype(F32)).astype(F32)
        total = total + jnp.sum(ones, axis=1, keepdims=True)
        member[:, here] = ones.astype(BF16)
    fold[...] = jnp.broadcast_to(jnp.maximum(total, 1.0), fold.shape)

    def lanes(block):
        return pl.ds(pl.multiple_of(block * LANES, LANES), LANES)

    def multiply(block, pairs, added):
        wide = jnp.concatenate([window[block], window[block + 1]], axis=1)
        for half in range(0, BAND, 2):
            cols = slice(half * LANES, (half + 2) * LANES)
            pairs[:, cols] = jnp.dot(wide, bands_ref[block, :, cols], preferred_element_type=F32)
        parts = list(split3(slow_ref[:, lanes(block)]))
        parts = [p.astype(F32) for p in parts + parts] + [jnp.zeros((LANES - 6 * bins, LANES), F32)]
        table = jnp.concatenate(parts, axis=0).astype(BF16)
        added[...] = jnp.dot(scaled[...], table, preferred_element_type=F32)

    def weigh(block, pairs, added, moved):
        ticks = iota((1, LANES), 1) + block * LANES
        time = ticks.astype(F32)
        squared = jnp.where(ticks == 0, 1e-30, time * time)
        start = start_ref[:, lanes(block)].astype(F32) + 3.5
        for row in range(0, items, STEP):
            here = slice(row, row + STEP)
            total = squared + added[here, :]
            lag = start - total * lax.rsqrt(total)
            value = correct(lag, lambda i: pairs[here, i * LANES : (i + 1) * LANES])
            high = value.astype(BF16)
            moved[here, :] = high
            moved[items + row : items + row + STEP, :] = (value - high.astype(F32)).astype(BF16)

    def total_up(block, moved):
        sums = jnp.dot(member[...], moved[:items, :], preferred_element_type=F32) + jnp.dot(
            member[...], moved[items:, :], preferred_element_type=F32
        )
        out_ref[:, lanes(block)] = sums / fold[...]

    multiply(0, pairs0, added0)

    def two_blocks(i, carry):
        block = 2 * i
        multiply(block + 1, pairs1, added1)
        weigh(block, pairs0, added0, moved0)
        total_up(jnp.maximum(block - 1, 0), moved1)
        multiply(jnp.minimum(block + 2, blocks - 1), pairs0, added0)
        weigh(block + 1, pairs1, added1, moved1)
        total_up(block, moved0)
        return carry

    lax.fori_loop(0, blocks // 2, two_blocks, 0)
    total_up(blocks - 1, moved1)
    width = first_ref.shape[0]
    height = bins // width
    for x in range(width):
        first_ref[x : x + 1, :] = out_ref[x * height : x * height + 1, :]
        last_ref[x : x + 1, :] = out_ref[(x + 1) * height - 1 : (x + 1) * height, :]


def stack(got, picks, band_start, slowness, rows_x):
    bins, samples = slowness.shape
    blocks = samples // LANES
    sources = got.shape[0] // ROWS
    items = CAP * sources
    edge = jax.ShapeDtypeStruct((rows_x, samples), F32)
    return pl.pallas_call(
        stack_kernel,
        in_specs=[VMEM] * 4,
        out_specs=[VMEM] * 3,
        out_shape=[jax.ShapeDtypeStruct((bins, samples), F32), edge, edge],
        scratch_shapes=[
            pltpu.VMEM((sources * PITCH, LANES), F32),
            pltpu.VMEM((blocks + 1, items, LANES), BF16),
            pltpu.VMEM((items, LANES), BF16),
            pltpu.VMEM((bins, items), BF16),
            pltpu.VMEM((bins, LANES), F32),
            pltpu.VMEM((items, BAND * LANES), F32),
            pltpu.VMEM((items, BAND * LANES), F32),
            pltpu.VMEM((items, LANES), F32),
            pltpu.VMEM((items, LANES), F32),
            pltpu.VMEM((2 * items, LANES), BF16),
            pltpu.VMEM((2 * items, LANES), BF16),
        ],
        compiler_params=pltpu.CompilerParams(vmem_limit_bytes=40 << 20),
        name="stack",
    )(got, picks, band_start.reshape(1, samples), slowness)


def edges_kernel(stack_ref, before_ref, after_ref, first_ref, last_ref):
    width = before_ref.shape[0]
    height = stack_ref.shape[0] // width
    for x, ref in ((0, first_ref), (width - 1, last_ref)):
        ref[0:1, :] = before_ref[x : x + 1, :]
        ref[1 : height + 1, :] = stack_ref[x * height : (x + 1) * height, :]
        ref[height + 1 : height + 2, :] = after_ref[x : x + 1, :]


def edges(stacked, before, after):
    rows_x, samples = before.shape
    edge = jax.ShapeDtypeStruct((stacked.shape[0] // rows_x + 2, samples), F32)
    return pl.pallas_call(
        edges_kernel,
        in_specs=[VMEM] * 3,
        out_specs=[VMEM] * 2,
        out_shape=[edge, edge],
        compiler_params=pltpu.CompilerParams(vmem_limit_bytes=8 << 20),
        name="edges",
    )(stacked, before, after)


def smooth_kernel(stack_ref, before_ref, after_ref, low_ref, high_ref, dip_ref, out_ref, padded):
    width = before_ref.shape[0]
    bins, samples = stack_ref.shape
    height = bins // width
    pitch = height + 2
    padded[0:pitch, :] = low_ref[...]
    for x in range(width):
        row = (x + 1) * pitch
        padded[row : row + 1, :] = before_ref[x : x + 1, :]
        padded[row + 1 : row + 1 + height, :] = stack_ref[x * height : (x + 1) * height, :]
        padded[row + 1 + height : row + pitch, :] = after_ref[x : x + 1, :]
    padded[(width + 1) * pitch : (width + 2) * pitch, :] = high_ref[...]
    near = []
    for n in range(9):
        dx, dy = n // 3, n % 3
        rows = [(dx + x) * pitch + dy for x in range(width)]
        near.append(jnp.concatenate([padded[r : r + height, :] for r in rows], axis=0))
    time = iota((bins, samples), 1)
    result = jnp.zeros((bins, samples), F32)
    for lag in range(-DIP, DIP + 1):
        part = jnp.zeros((bins, samples), F32)
        for n in range(9):
            factor = CENTER_WEIGHT if n == 4 else SIDE_WEIGHT
            weight = jnp.where(dip_ref[:, n : n + 1] == lag, factor, 0.0)
            part = part + weight * near[n]
        if lag:
            part = pltpu.roll(part, (-lag) % samples, 1)
            part = jnp.where((time + lag >= 0) & (time + lag < samples), part, 0.0)
        result = result + part
    for x in range(width):
        out_ref[x] = result[x * height : (x + 1) * height, :]


def smooth(stacked, before, after, low, high, dip):
    rows_x, samples = before.shape
    bins = stacked.shape[0]
    rows_y = bins // rows_x
    return pl.pallas_call(
        smooth_kernel,
        in_specs=[VMEM] * 6,
        out_specs=VMEM,
        out_shape=jax.ShapeDtypeStruct((rows_x, rows_y, samples), F32),
        scratch_shapes=[pltpu.VMEM(((rows_x + 2) * (rows_y + 2), samples), F32)],
        compiler_params=pltpu.CompilerParams(vmem_limit_bytes=8 << 20),
        name="smooth",
    )(stacked, before, after, low, high, dip)


def exchange(first, last, axis):
    size = lax.axis_size(axis)
    before = lax.ppermute(last, axis, [(i, i + 1) for i in range(size - 1)])
    after = lax.ppermute(first, axis, [(i + 1, i) for i in range(size - 1)])
    return before, after


def body(traces, trace_offset, trace_owner, trace_cell, slowness, band_start, dip_shift):
    owners = lax.axis_size(AXES)
    rows_x, rows_y, samples = slowness.shape
    bins = rows_x * rows_y
    send = dispatch(traces, trace_owner, trace_cell, trace_offset, owners)
    got = lax.all_to_all(send.reshape(owners, ROWS, LANES), AXES, split_axis=0, concat_axis=0, tiled=True)
    picks = bands(band_start)
    stacked, first, last = stack(
        got.reshape(owners * ROWS, LANES), picks, band_start, slowness.reshape(bins, samples), rows_x
    )
    before, after = exchange(first, last, "iline")
    low, high = exchange(*edges(stacked, before, after), "xline")
    return smooth(stacked, before, after, low, high, dip_shift.reshape(9, bins).T)


def solution(mesh):
    return jax.shard_map(
        body,
        mesh=mesh,
        in_specs=(
            P(AXES, None),
            P(AXES),
            P(AXES),
            P(AXES),
            P("xline", "iline", None),
            P(),
            P(None, "xline", "iline"),
        ),
        out_specs=P("xline", "iline", None),
        check_vma=False,
    )
```

```python
import functools

import jax
import jax.numpy as jnp
from jax import lax
from jax.experimental import pallas as pl
from jax.experimental.pallas import tpu as pltpu
from jax.sharding import PartitionSpec as P

BAND = 8
DIP = 4
REACH = BAND - 1
LANES = 128
CAP = 5
ROWS = 64
PITCH = 65
STEP = 32
HALVES = (0.5, 1.5, 2.5, 3.5)
VMEM = pl.BlockSpec(memory_space=pltpu.VMEM)
HBM = pl.BlockSpec(memory_space=pltpu.HBM)

CENTER_WEIGHT = 0.5
SIDE_WEIGHT = 0.0625

AXES = ("xline", "iline")
F32 = jnp.float32
BF16 = jnp.bfloat16


def iota(shape, dim):
    return lax.broadcasted_iota(jnp.int32, shape, dim)


def in_line(value):
    return jnp.concatenate([value[i : i + 1, :] for i in range(value.shape[0])], axis=1)


def dispatch_kernel(owners, traces_hbm, owner_hbm, cell_hbm, offset_hbm, out_ref, traces_ref, owner_ref, cell_ref, offset_ref, stage, arrived):
    pairs = ((owner_hbm, owner_ref), (cell_hbm, cell_ref), (offset_hbm, offset_ref), (traces_hbm, traces_ref))
    copies = [pltpu.make_async_copy(there, here, arrived.at[i]) for i, (there, here) in enumerate(pairs)]
    for copy in copies:
        copy.start()
    rows, samples = traces_ref.shape
    blocks = samples // LANES
    for copy in copies[:3]:
        copy.wait()
    owner = in_line(owner_ref[...])
    hot = (iota((owners, rows), 0) == owner).astype(F32)
    earlier = (iota((rows, rows), 0) < iota((rows, rows), 1)).astype(F32).astype(BF16)
    counts = jnp.dot(hot.astype(BF16), earlier, preferred_element_type=F32)
    rank = jnp.sum(hot * counts, axis=0, keepdims=True)
    picks = [jnp.where(rank == float(k), hot, 0.0).astype(BF16) for k in range(CAP)]
    pick = jnp.concatenate(picks, axis=0)
    meta = jnp.zeros((owners, LANES), F32)
    line = iota((LANES, rows), 0)
    offset = in_line(offset_ref[...].astype(F32))
    cell = in_line(cell_ref[...] + 1).astype(F32)
    for k in range(CAP):
        source = jnp.where(line == 8 * k, offset, jnp.where(line == 8 * k + 1, cell, 0.0))
        meta = meta + lax.dot_general(
            picks[k], source.astype(BF16), (((1,), (1,)), ((), ())), preferred_element_type=F32
        )
    stage[pl.ds(CAP * blocks, owners, stride=PITCH), :] = meta
    for row in range(CAP * blocks + 1, ROWS):
        stage[pl.ds(row, owners, stride=PITCH), :] = jnp.zeros((owners, LANES), F32)
    copies[3].wait()
    wrapped = iota((CAP * owners, LANES), 1) < REACH

    def put(block, value):
        for k in range(CAP):
            stage[pl.ds(k * blocks + block, owners, stride=PITCH), :] = value[k * owners : (k + 1) * owners, :]

    first = previous = None
    for tile in range(0, samples, 2 * LANES):
        placed = jnp.dot(pick, traces_ref[:, tile : tile + 2 * LANES], preferred_element_type=F32)
        for half in range(2):
            turned = pltpu.roll(placed[:, half * LANES : (half + 1) * LANES], REACH, 1)
            if first is None:
                first = turned
            else:
                put(tile // LANES + half, jnp.where(wrapped, previous, turned))
            previous = turned
    put(0, jnp.where(wrapped, previous, first))
    for owner_row in range(owners):
        out_ref[owner_row * ROWS : (owner_row + 1) * ROWS, :] = stage[
            owner_row * PITCH : owner_row * PITCH + ROWS, :
        ].astype(BF16)


def dispatch(traces, owner, cell, offset, owners):
    rows, samples = traces.shape
    return pl.pallas_call(
        functools.partial(dispatch_kernel, owners),
        in_specs=[HBM] * 4,
        out_specs=VMEM,
        out_shape=jax.ShapeDtypeStruct((owners * ROWS, LANES), BF16),
        scratch_shapes=[
            pltpu.VMEM((rows, samples), BF16),
            pltpu.VMEM((rows // LANES, LANES), jnp.int32),
            pltpu.VMEM((rows // LANES, LANES), jnp.int32),
            pltpu.VMEM((rows // LANES, LANES), BF16),
            pltpu.VMEM((owners * PITCH, LANES), F32),
            pltpu.SemaphoreType.DMA((4,)),
        ],
        name="dispatch",
    )(traces, *(v.reshape(rows // LANES, LANES) for v in (owner, cell, offset)))


def bands_kernel(start_ref, out_ref):
    first = start_ref[...] + (REACH - pl.program_id(0) * LANES)
    place = iota((2 * LANES, LANES), 0) - first
    for i, half in enumerate(HALVES):
        low = (place == int(3.5 - half)).astype(F32)
        high = (place == int(3.5 + half)).astype(F32)
        out_ref[0, :, i * LANES : (i + 1) * LANES] = (0.5 * (low + high)).astype(BF16)
        out_ref[0, :, (4 + i) * LANES : (5 + i) * LANES] = (half * (low - high)).astype(BF16)


def bands(band_start):
    samples = band_start.shape[0]
    blocks = samples // LANES
    return pl.pallas_call(
        bands_kernel,
        grid=(blocks,),
        in_specs=[pl.BlockSpec((1, LANES), lambda b: (0, b))],
        out_specs=pl.BlockSpec((1, 2 * LANES, BAND * LANES), lambda b: (b, 0, 0)),
        out_shape=jax.ShapeDtypeStruct((blocks, 2 * LANES, BAND * LANES), BF16),
        name="bands",
    )(band_start.reshape(1, samples))


def split3(value):
    high = value.astype(BF16)
    rest = value - high.astype(F32)
    middle = rest.astype(BF16)
    low = (rest - middle.astype(F32)).astype(BF16)
    return high, middle, low


def correct(lag, band):
    square = lag * lag
    num = odd = den = None
    for i, half in enumerate(HALVES):
        near = square + (1.0 + half * half)
        if half == 0.5:
            prod = near * near - square
        else:
            prod = (square + (2.0 - 2.0 * half * half)) * square + (1.0 + half * half) ** 2
        both = 1.0 / prod
        share = near * both
        part, tilt = band(i) * share, band(4 + i) * both
        num, odd, den = (part, tilt, share) if num is None else (num + part, odd + tilt, den + share)
    return (num + lag * odd) / den


def stack_kernel(got_ref, bands_hbm, start_ref, slow_ref, out_ref, first_ref, last_ref, stage, bands_ref, window, scaled, member, fold, pairs0, pairs1, added0, added1, moved0, moved1, arrived):
    blocks = bands_hbm.shape[0]

    def fetch(block):
        return pltpu.make_async_copy(bands_hbm.at[block], bands_ref.at[block], arrived.at[block])

    for block in range(blocks):
        fetch(block).start()
    bins = slow_ref.shape[0]
    sources = got_ref.shape[0] // ROWS
    items = CAP * sources
    for src in range(sources):
        stage[src * PITCH : src * PITCH + ROWS, :] = got_ref[src * ROWS : (src + 1) * ROWS, :].astype(F32)
    meta = stage[pl.ds(CAP * blocks, sources, stride=PITCH), :]
    across = meta.T
    lane = iota((sources, LANES), 1)
    total = jnp.zeros((bins, 1), F32)
    for k in range(CAP):
        here = slice(k * sources, (k + 1) * sources)
        for b in range(blocks):
            rows = stage[pl.ds(k * blocks + b, sources, stride=PITCH), :].astype(BF16)
            window[b, here, :] = rows
            if b == 0:
                window[blocks, here, :] = rows
        offset = meta[:, 8 * k : 8 * k + 1]
        cell = meta[:, 8 * k + 1 : 8 * k + 2] - 1.0
        square = offset * offset
        high = square.astype(BF16).astype(F32)
        part = jnp.where(lane < 3 * bins, high, square - high)
        keep = ((lane % bins).astype(F32) == cell) & (lane < 6 * bins)
        scaled[here, :] = jnp.where(keep, part, 0.0).astype(BF16)
        ones = (across[8 * k + 1 : 8 * k + 2, :] == (iota((bins, sources), 0) + 1).astype(F32)).astype(F32)
        total = total + jnp.sum(ones, axis=1, keepdims=True)
        member[:, here] = ones.astype(BF16)
    fold[...] = jnp.broadcast_to(jnp.maximum(total, 1.0), fold.shape)

    def lanes(block):
        return slice(block * LANES, (block + 1) * LANES)

    def multiply(block, pairs, added):
        wide = jnp.concatenate([window[block], window[block + 1]], axis=1)

        def shift():
            parts = list(split3(slow_ref[:, lanes(block)]))
            parts = [p.astype(F32) for p in parts + parts] + [jnp.zeros((LANES - 6 * bins, LANES), F32)]
            table = jnp.concatenate(parts, axis=0).astype(BF16)
            added[...] = jnp.dot(scaled[...], table, preferred_element_type=F32)

        def pick(half):
            cols = slice(half * LANES, (half + 2) * LANES)
            pairs[:, cols] = jnp.dot(wide, bands_ref[block, :, cols], preferred_element_type=F32)

        return [shift] + [functools.partial(pick, half) for half in range(0, BAND, 2)]

    def weigh(block, pairs, added, moved):
        ticks = iota((1, LANES), 1) + block * LANES
        time = ticks.astype(F32)
        squared = jnp.where(ticks == 0, 1e-30, time * time)
        start = start_ref[:, lanes(block)].astype(F32) + 3.5

        def chunk(row):
            here = slice(row, row + STEP)
            total = squared + added[here, :]
            lag = start - total * lax.rsqrt(total)
            value = correct(lag, lambda i: pairs[here, i * LANES : (i + 1) * LANES])
            high = value.astype(BF16)
            moved[here, :] = high
            moved[items + row : items + row + STEP, :] = (value - high.astype(F32)).astype(BF16)

        return [functools.partial(chunk, row) for row in range(0, items, STEP)]

    def total_up(block, moved):
        sums = jnp.dot(member[...], moved[:items, :], preferred_element_type=F32) + jnp.dot(
            member[...], moved[items:, :], preferred_element_type=F32
        )
        out_ref[:, lanes(block)] = sums / fold[...]

    def interleave(few, many):
        for i, work in enumerate(many):
            for j, other in enumerate(few):
                if j * len(many) // len(few) == i:
                    other()
            work()

    for block in range(blocks):
        fetch(block).wait()
    for work in multiply(0, pairs0, added0):
        work()

    pairs, added, moved = (pairs0, pairs1), (added0, added1), (moved0, moved1)
    for block in range(blocks):
        now, later = block % 2, (block + 1) % 2
        ahead = []
        if block + 1 < blocks:
            ahead = multiply(block + 1, pairs[later], added[later])
        if block:
            total_up(block - 1, moved[later])
        interleave(ahead, weigh(block, pairs[now], added[now], moved[now]))
    total_up(blocks - 1, moved[(blocks - 1) % 2])
    first_ref[...] = out_ref[: first_ref.shape[0], :]
    last_ref[...] = out_ref[bins - last_ref.shape[0] :, :]


def stack(got, picks, band_start, slowness, rows_y):
    bins, samples = slowness.shape
    blocks = samples // LANES
    sources = got.shape[0] // ROWS
    items = CAP * sources
    edge = jax.ShapeDtypeStruct((rows_y, samples), F32)
    return pl.pallas_call(
        stack_kernel,
        in_specs=[VMEM, HBM, VMEM, VMEM],
        out_specs=[VMEM] * 3,
        out_shape=[jax.ShapeDtypeStruct((bins, samples), F32), edge, edge],
        scratch_shapes=[
            pltpu.VMEM((sources * PITCH, LANES), F32),
            pltpu.VMEM((blocks, 2 * LANES, BAND * LANES), BF16),
            pltpu.VMEM((blocks + 1, items, LANES), BF16),
            pltpu.VMEM((items, LANES), BF16),
            pltpu.VMEM((bins, items), BF16),
            pltpu.VMEM((bins, LANES), F32),
            pltpu.VMEM((items, BAND * LANES), F32),
            pltpu.VMEM((items, BAND * LANES), F32),
            pltpu.VMEM((items, LANES), F32),
            pltpu.VMEM((items, LANES), F32),
            pltpu.VMEM((2 * items, LANES), BF16),
            pltpu.VMEM((2 * items, LANES), BF16),
            pltpu.SemaphoreType.DMA((blocks,)),
        ],
        compiler_params=pltpu.CompilerParams(vmem_limit_bytes=40 << 20),
        name="stack",
    )(got, picks, band_start.reshape(1, samples), slowness)


def edges_kernel(stack_ref, low_ref, high_ref, first_ref, last_ref):
    height = low_ref.shape[0]
    width = stack_ref.shape[0] // height
    for y, ref in ((0, first_ref), (height - 1, last_ref)):
        ref[0:1, :] = low_ref[y : y + 1, :]
        for x in range(width):
            ref[x + 1 : x + 2, :] = stack_ref[x * height + y : x * height + y + 1, :]
        ref[width + 1 : width + 2, :] = high_ref[y : y + 1, :]


def edges(stacked, low, high):
    rows_y, samples = low.shape
    edge = jax.ShapeDtypeStruct((stacked.shape[0] // rows_y + 2, samples), F32)
    return pl.pallas_call(
        edges_kernel,
        in_specs=[VMEM] * 3,
        out_specs=[VMEM] * 2,
        out_shape=[edge, edge],
        compiler_params=pltpu.CompilerParams(vmem_limit_bytes=8 << 20),
        name="edges",
    )(stacked, low, high)


def smooth_kernel(stack_ref, low_ref, high_ref, before_ref, after_ref, dip_ref, out_ref, padded):
    height = low_ref.shape[0]
    bins, samples = stack_ref.shape
    width = bins // height
    pitch = height + 2
    for x in range(width + 2):
        row = x * pitch
        padded[row : row + 1, :] = before_ref[x : x + 1, :]
        if x == 0:
            inner = low_ref[...]
        elif x == width + 1:
            inner = high_ref[...]
        else:
            inner = stack_ref[(x - 1) * height : x * height, :]
        padded[row + 1 : row + 1 + height, :] = inner
        padded[row + 1 + height : row + pitch, :] = after_ref[x : x + 1, :]
    across, down = iota(dip_ref.shape, 1), iota(dip_ref.shape, 0)
    bin_x = lax.axis_index("xline") * width + down // height + across // 3 - 1
    bin_y = lax.axis_index("iline") * height + down % height + across % 3 - 1
    limit_x, limit_y = lax.axis_size("xline") * width, lax.axis_size("iline") * height
    inside = (bin_x >= 0) & (bin_x < limit_x) & (bin_y >= 0) & (bin_y < limit_y)
    dip = jnp.where(inside, dip_ref[...], 2 * DIP + 1)
    near = []
    for n in range(9):
        dx, dy = n // 3, n % 3
        rows = [(dx + x) * pitch + dy for x in range(width)]
        near.append(jnp.concatenate([padded[r : r + height, :] for r in rows], axis=0))
    time = iota((bins, samples), 1)
    result = jnp.zeros((bins, samples), F32)
    for lag in range(-DIP, DIP + 1):
        part = jnp.zeros((bins, samples), F32)
        for n in range(9):
            factor = CENTER_WEIGHT if n == 4 else SIDE_WEIGHT
            weight = jnp.where(dip[:, n : n + 1] == lag, factor, 0.0)
            part = part + weight * near[n]
        if lag:
            part = pltpu.roll(part, (-lag) % samples, 1)
            part = jnp.where((time + lag >= 0) & (time + lag < samples), part, 0.0)
        result = result + part
    for x in range(width):
        out_ref[x] = result[x * height : (x + 1) * height, :]


def smooth(stacked, low, high, before, after, dip):
    rows_y, samples = low.shape
    bins = stacked.shape[0]
    rows_x = bins // rows_y
    return pl.pallas_call(
        smooth_kernel,
        in_specs=[VMEM] * 6,
        out_specs=VMEM,
        out_shape=jax.ShapeDtypeStruct((rows_x, rows_y, samples), F32),
        scratch_shapes=[pltpu.VMEM(((rows_x + 2) * (rows_y + 2), samples), F32)],
        compiler_params=pltpu.CompilerParams(vmem_limit_bytes=8 << 20),
        name="smooth",
    )(stacked, low, high, before, after, dip)


def exchange(first, last, axis):
    size = lax.axis_size(axis)
    before = lax.ppermute(last, axis, [(i, (i + 1) % size) for i in range(size)])
    after = lax.ppermute(first, axis, [((i + 1) % size, i) for i in range(size)])
    return before, after


def body(traces, trace_offset, trace_owner, trace_cell, slowness, band_start, dip_shift):
    owners = lax.axis_size(AXES)
    rows_x, rows_y, samples = slowness.shape
    bins = rows_x * rows_y
    send = dispatch(traces, trace_owner, trace_cell, trace_offset, owners)
    got = lax.all_to_all(send.reshape(owners, ROWS, LANES), AXES, split_axis=0, concat_axis=0, tiled=True)
    picks = pltpu.with_memory_space_constraint(bands(band_start), pltpu.HBM)
    stacked, first, last = stack(
        got.reshape(owners * ROWS, LANES), picks, band_start, slowness.reshape(bins, samples), rows_y
    )
    low, high = exchange(first, last, "xline")
    before, after = exchange(*edges(stacked, low, high), "iline")
    return smooth(stacked, low, high, before, after, dip_shift.reshape(9, bins).T)


def solution(mesh):
    return jax.shard_map(
        body,
        mesh=mesh,
        in_specs=(
            P(AXES, None),
            P(AXES),
            P(AXES),
            P(AXES),
            P("xline", "iline", None),
            P(),
            P(None, "xline", "iline"),
        ),
        out_specs=P("xline", "iline", None),
        check_vma=False,
    )
```

```python
import functools

import jax
import jax.numpy as jnp
from jax import lax
from jax.experimental import pallas as pl
from jax.experimental.pallas import tpu as pltpu
from jax.sharding import PartitionSpec as P

BAND = 8
DIP = 4
REACH = BAND - 1
LANES = 128
CAP = 5
ROWS = 62
PARTS = 4
REACHED = 144
STEP = 32
HALVES = (0.5, 1.5, 2.5, 3.5)
VMEM = pl.BlockSpec(memory_space=pltpu.VMEM)
HBM = pl.BlockSpec(memory_space=pltpu.HBM)

CENTER_WEIGHT = 0.5
SIDE_WEIGHT = 0.0625

AXES = ("xline", "iline")
F32 = jnp.float32
BF16 = jnp.bfloat16


def iota(shape, dim):
    return lax.broadcasted_iota(jnp.int32, shape, dim)


def in_line(value):
    return jnp.concatenate([value[i : i + 1, :] for i in range(value.shape[0])], axis=1)


def dispatch_kernel(owners, traces_hbm, owner_hbm, cell_hbm, offset_hbm, out_ref, traces_ref, owner_ref, cell_ref, offset_ref, stage, packed, arrived, sent):
    pairs = ((owner_hbm, owner_ref), (cell_hbm, cell_ref), (offset_hbm, offset_ref), (traces_hbm, traces_ref))
    copies = [pltpu.make_async_copy(there, here, arrived.at[i]) for i, (there, here) in enumerate(pairs)]
    for copy in copies:
        copy.start()
    rows, samples = traces_ref.shape
    blocks = samples // LANES
    for copy in copies[:3]:
        copy.wait()
    owner = in_line(owner_ref[...])
    hot = (iota((owners, rows), 0) == owner).astype(F32)
    earlier = (iota((rows, rows), 0) < iota((rows, rows), 1)).astype(F32).astype(BF16)
    counts = jnp.dot(hot.astype(BF16), earlier, preferred_element_type=F32)
    rank = jnp.sum(hot * counts, axis=0, keepdims=True)
    picks = [jnp.where(rank == float(k), hot, 0.0).astype(BF16) for k in range(CAP)]
    pick = jnp.concatenate(picks, axis=0)
    meta = jnp.zeros((owners, LANES), F32)
    line = iota((LANES, rows), 0)
    offset = in_line(offset_ref[...].astype(F32))
    cell = in_line(cell_ref[...] + 1).astype(F32)
    for k in range(CAP):
        source = jnp.where(line == 8 * k, offset, jnp.where(line == 8 * k + 1, cell, 0.0))
        meta = meta + lax.dot_general(
            picks[k], source.astype(BF16), (((1,), (1,)), ((), ())), preferred_element_type=F32
        )
    stage[pl.ds(CAP * blocks, owners, stride=ROWS), :] = meta
    for row in range(CAP * blocks + 1, ROWS):
        stage[pl.ds(row, owners, stride=ROWS), :] = jnp.zeros((owners, LANES), F32)
    copies[3].wait()
    wrapped = iota((CAP * owners, LANES), 1) < REACH

    def put(block, value):
        for k in range(CAP):
            stage[pl.ds(k * blocks + block, owners, stride=ROWS), :] = value[k * owners : (k + 1) * owners, :]

    first = previous = None
    for tile in range(0, samples, 2 * LANES):
        placed = jnp.dot(pick, traces_ref[:, tile : tile + 2 * LANES], preferred_element_type=F32)
        for half in range(2):
            turned = pltpu.roll(placed[:, half * LANES : (half + 1) * LANES], REACH, 1)
            if first is None:
                first = turned
            else:
                put(tile // LANES + half, jnp.where(wrapped, previous, turned))
            previous = turned
    put(0, jnp.where(wrapped, previous, first))
    size = owners * ROWS // PARTS
    sends = []
    for part in range(PARTS):
        here = pl.ds(part * size, size)
        packed[here, :] = stage[here, :].astype(BF16)
        sends.append(pltpu.make_async_copy(packed.at[here, :], out_ref.at[here, :], sent.at[part]))
        sends[-1].start()
    for copy in sends:
        copy.wait()


def dispatch(traces, owner, cell, offset, owners):
    rows, samples = traces.shape
    return pl.pallas_call(
        functools.partial(dispatch_kernel, owners),
        in_specs=[HBM] * 4,
        out_specs=HBM,
        out_shape=jax.ShapeDtypeStruct((owners * ROWS, LANES), BF16),
        scratch_shapes=[
            pltpu.VMEM((rows, samples), BF16),
            pltpu.VMEM((rows // LANES, LANES), jnp.int32),
            pltpu.VMEM((rows // LANES, LANES), jnp.int32),
            pltpu.VMEM((rows // LANES, LANES), BF16),
            pltpu.VMEM((owners * ROWS, LANES), F32),
            pltpu.VMEM((owners * ROWS, LANES), BF16),
            pltpu.SemaphoreType.DMA((4,)),
            pltpu.SemaphoreType.DMA((PARTS,)),
        ],
        name="dispatch",
    )(traces, *(v.reshape(rows // LANES, LANES) for v in (owner, cell, offset)))


def bands_kernel(start_ref, out_ref):
    first = start_ref[...] + (REACH - pl.program_id(0) * LANES)
    place = iota((REACHED, LANES), 0) - first
    for i, half in enumerate(HALVES):
        low = (place == int(3.5 - half)).astype(F32)
        high = (place == int(3.5 + half)).astype(F32)
        out_ref[0, :, i * LANES : (i + 1) * LANES] = (0.5 * (low + high)).astype(BF16)
        out_ref[0, :, (4 + i) * LANES : (5 + i) * LANES] = (half * (low - high)).astype(BF16)


def bands(band_start):
    samples = band_start.shape[0]
    blocks = samples // LANES
    return pl.pallas_call(
        bands_kernel,
        grid=(blocks,),
        in_specs=[pl.BlockSpec((1, LANES), lambda b: (0, b))],
        out_specs=pl.BlockSpec((1, REACHED, BAND * LANES), lambda b: (b, 0, 0)),
        out_shape=jax.ShapeDtypeStruct((blocks, REACHED, BAND * LANES), BF16),
        name="bands",
    )(band_start.reshape(1, samples))


def split3(value):
    high = value.astype(BF16)
    rest = value - high.astype(F32)
    middle = rest.astype(BF16)
    low = (rest - middle.astype(F32)).astype(BF16)
    return high, middle, low


def correct(lag, band):
    square = lag * lag
    num = odd = den = None
    for i, half in enumerate(HALVES):
        near = square + (1.0 + half * half)
        if half == 0.5:
            prod = near * near - square
        else:
            prod = (square + (2.0 - 2.0 * half * half)) * square + (1.0 + half * half) ** 2
        both = 1.0 / prod
        share = near * both
        part, tilt = band(i) * share, band(4 + i) * both
        num, odd, den = (part, tilt, share) if num is None else (num + part, odd + tilt, den + share)
    return (num + lag * odd) / den


def stack_kernel(got_ref, bands_hbm, start_ref, slow_ref, out_ref, first_ref, last_ref, stage, bands_ref, window, scaled, member, fold, pairs0, pairs1, added0, added1, moved0, moved1, arrived):
    blocks = bands_hbm.shape[0]

    def fetch(block):
        return pltpu.make_async_copy(bands_hbm.at[block], bands_ref.at[block], arrived.at[block])

    for block in range(blocks):
        fetch(block).start()
    bins = slow_ref.shape[0]
    sources = got_ref.shape[0] // ROWS
    items = CAP * sources
    stage[...] = got_ref[...].astype(F32)
    meta = stage[pl.ds(CAP * blocks, sources, stride=ROWS), :]
    across = meta.T
    lane = iota((sources, LANES), 1)
    total = jnp.zeros((bins, 1), F32)
    for k in range(CAP):
        here = slice(k * sources, (k + 1) * sources)
        offset = meta[:, 8 * k : 8 * k + 1]
        cell = meta[:, 8 * k + 1 : 8 * k + 2] - 1.0
        square = offset * offset
        high = square.astype(BF16).astype(F32)
        part = jnp.where(lane < 3 * bins, high, square - high)
        keep = ((lane % bins).astype(F32) == cell) & (lane < 6 * bins)
        scaled[here, :] = jnp.where(keep, part, 0.0).astype(BF16)
        ones = (across[8 * k + 1 : 8 * k + 2, :] == (iota((bins, sources), 0) + 1).astype(F32)).astype(F32)
        total = total + jnp.sum(ones, axis=1, keepdims=True)
        member[:, here] = ones.astype(BF16)
    fold[...] = jnp.broadcast_to(jnp.maximum(total, 1.0), fold.shape)

    def gather(block):
        for k in range(CAP):
            rows = stage[pl.ds(k * blocks + block % blocks, sources, stride=ROWS), :]
            window[block, k * sources : (k + 1) * sources, :] = rows.astype(BF16)

    def lanes(block):
        return slice(block * LANES, (block + 1) * LANES)

    def multiply(block, pairs, added):
        wide = jnp.concatenate([window[block], window[block + 1]], axis=1)

        def shift():
            parts = list(split3(slow_ref[:, lanes(block)]))
            parts = [p.astype(F32) for p in parts + parts] + [jnp.zeros((LANES - 6 * bins, LANES), F32)]
            table = jnp.concatenate(parts, axis=0).astype(BF16)
            added[...] = jnp.dot(scaled[...], table, preferred_element_type=F32)

        def pick(half):
            cols = slice(half * LANES, (half + 2) * LANES)
            rows = jnp.concatenate([bands_ref[block, :, cols], jnp.zeros((2 * LANES - REACHED, 2 * LANES), BF16)], axis=0)
            pairs[:, cols] = jnp.dot(wide, rows, preferred_element_type=F32)

        return [shift] + [functools.partial(pick, half) for half in range(0, BAND, 2)]

    def weigh(block, pairs, added, moved):
        ticks = iota((1, LANES), 1) + block * LANES
        time = ticks.astype(F32)
        squared = jnp.where(ticks == 0, 1e-30, time * time)
        start = start_ref[:, lanes(block)].astype(F32) + 3.5

        def chunk(row):
            here = slice(row, row + STEP)
            total = squared + added[here, :]
            lag = start - total * lax.rsqrt(total)
            value = correct(lag, lambda i: pairs[here, i * LANES : (i + 1) * LANES])
            high = value.astype(BF16)
            moved[here, :] = high
            moved[items + row : items + row + STEP, :] = (value - high.astype(F32)).astype(BF16)

        return [functools.partial(chunk, row) for row in range(0, items, STEP)]

    def total_up(block, moved):
        sums = jnp.dot(member[...], moved[:items, :], preferred_element_type=F32) + jnp.dot(
            member[...], moved[items:, :], preferred_element_type=F32
        )
        out_ref[:, lanes(block)] = sums / fold[...]

    def interleave(few, many):
        for i, work in enumerate(many):
            for j, other in enumerate(few):
                if j * len(many) // len(few) == i:
                    other()
            work()

    for block in range(blocks):
        fetch(block).wait()
    gather(0)
    gather(1)
    for work in multiply(0, pairs0, added0):
        work()

    pairs, added, moved = (pairs0, pairs1), (added0, added1), (moved0, moved1)
    for block in range(blocks):
        now, later = block % 2, (block + 1) % 2
        ahead = []
        if block + 1 < blocks:
            gather(block + 2)
            ahead = multiply(block + 1, pairs[later], added[later])
        if block:
            total_up(block - 1, moved[later])
        interleave(ahead, weigh(block, pairs[now], added[now], moved[now]))
    total_up(blocks - 1, moved[(blocks - 1) % 2])
    first_ref[...] = out_ref[: first_ref.shape[0], :]
    last_ref[...] = out_ref[bins - last_ref.shape[0] :, :]


def stack(got, picks, band_start, slowness, rows_y):
    bins, samples = slowness.shape
    blocks = samples // LANES
    sources = got.shape[0] // ROWS
    items = CAP * sources
    edge = jax.ShapeDtypeStruct((rows_y, samples), F32)
    return pl.pallas_call(
        stack_kernel,
        in_specs=[VMEM, HBM, VMEM, VMEM],
        out_specs=[VMEM] * 3,
        out_shape=[jax.ShapeDtypeStruct((bins, samples), F32), edge, edge],
        scratch_shapes=[
            pltpu.VMEM((sources * ROWS, LANES), F32),
            pltpu.VMEM((blocks, REACHED, BAND * LANES), BF16),
            pltpu.VMEM((blocks + 1, items, LANES), BF16),
            pltpu.VMEM((items, LANES), BF16),
            pltpu.VMEM((bins, items), BF16),
            pltpu.VMEM((bins, LANES), F32),
            pltpu.VMEM((items, BAND * LANES), F32),
            pltpu.VMEM((items, BAND * LANES), F32),
            pltpu.VMEM((items, LANES), F32),
            pltpu.VMEM((items, LANES), F32),
            pltpu.VMEM((2 * items, LANES), BF16),
            pltpu.VMEM((2 * items, LANES), BF16),
            pltpu.SemaphoreType.DMA((blocks,)),
        ],
        compiler_params=pltpu.CompilerParams(vmem_limit_bytes=40 << 20),
        name="stack",
    )(got, picks, band_start.reshape(1, samples), slowness)


def edges_kernel(stack_ref, low_ref, high_ref, first_ref, last_ref):
    height = low_ref.shape[0]
    width = stack_ref.shape[0] // height
    for y, ref in ((0, first_ref), (height - 1, last_ref)):
        ref[0:1, :] = low_ref[y : y + 1, :]
        for x in range(width):
            ref[x + 1 : x + 2, :] = stack_ref[x * height + y : x * height + y + 1, :]
        ref[width + 1 : width + 2, :] = high_ref[y : y + 1, :]


def edges(stacked, low, high):
    rows_y, samples = low.shape
    edge = jax.ShapeDtypeStruct((stacked.shape[0] // rows_y + 2, samples), F32)
    return pl.pallas_call(
        edges_kernel,
        in_specs=[VMEM] * 3,
        out_specs=[VMEM] * 2,
        out_shape=[edge, edge],
        compiler_params=pltpu.CompilerParams(vmem_limit_bytes=8 << 20),
        name="edges",
    )(stacked, low, high)


def smooth_kernel(stack_ref, low_ref, high_ref, before_ref, after_ref, dip_ref, out_ref, padded):
    height = low_ref.shape[0]
    bins, samples = stack_ref.shape
    width = bins // height
    pitch = height + 2
    for x in range(width + 2):
        row = x * pitch
        padded[row : row + 1, :] = before_ref[x : x + 1, :]
        if x == 0:
            inner = low_ref[...]
        elif x == width + 1:
            inner = high_ref[...]
        else:
            inner = stack_ref[(x - 1) * height : x * height, :]
        padded[row + 1 : row + 1 + height, :] = inner
        padded[row + 1 + height : row + pitch, :] = after_ref[x : x + 1, :]
    across, down = iota(dip_ref.shape, 1), iota(dip_ref.shape, 0)
    bin_x = lax.axis_index("xline") * width + down // height + across // 3 - 1
    bin_y = lax.axis_index("iline") * height + down % height + across % 3 - 1
    limit_x, limit_y = lax.axis_size("xline") * width, lax.axis_size("iline") * height
    inside = (bin_x >= 0) & (bin_x < limit_x) & (bin_y >= 0) & (bin_y < limit_y)
    dip = jnp.where(inside, dip_ref[...], 2 * DIP + 1)
    near = []
    for n in range(9):
        dx, dy = n // 3, n % 3
        rows = [(dx + x) * pitch + dy for x in range(width)]
        near.append(jnp.concatenate([padded[r : r + height, :] for r in rows], axis=0))
    time = iota((bins, samples), 1)
    result = jnp.zeros((bins, samples), F32)
    for lag in range(-DIP, DIP + 1):
        part = jnp.zeros((bins, samples), F32)
        for n in range(9):
            factor = CENTER_WEIGHT if n == 4 else SIDE_WEIGHT
            weight = jnp.where(dip[:, n : n + 1] == lag, factor, 0.0)
            part = part + weight * near[n]
        if lag:
            part = pltpu.roll(part, (-lag) % samples, 1)
            part = jnp.where((time + lag >= 0) & (time + lag < samples), part, 0.0)
        result = result + part
    for x in range(width):
        out_ref[x] = result[x * height : (x + 1) * height, :]


def smooth(stacked, low, high, before, after, dip):
    rows_y, samples = low.shape
    bins = stacked.shape[0]
    rows_x = bins // rows_y
    return pl.pallas_call(
        smooth_kernel,
        in_specs=[VMEM] * 6,
        out_specs=VMEM,
        out_shape=jax.ShapeDtypeStruct((rows_x, rows_y, samples), F32),
        scratch_shapes=[pltpu.VMEM(((rows_x + 2) * (rows_y + 2), samples), F32)],
        compiler_params=pltpu.CompilerParams(vmem_limit_bytes=8 << 20),
        name="smooth",
    )(stacked, low, high, before, after, dip)


def exchange(first, last, axis):
    size = lax.axis_size(axis)
    before = lax.ppermute(last, axis, [(i, (i + 1) % size) for i in range(size)])
    after = lax.ppermute(first, axis, [((i + 1) % size, i) for i in range(size)])
    return before, after


def body(traces, trace_offset, trace_owner, trace_cell, slowness, band_start, dip_shift):
    owners = lax.axis_size(AXES)
    rows_x, rows_y, samples = slowness.shape
    bins = rows_x * rows_y
    send = dispatch(traces, trace_owner, trace_cell, trace_offset, owners)
    send = send.reshape(owners, ROWS // 2, 2, LANES)
    got = lax.all_to_all(send, AXES, split_axis=0, concat_axis=0, tiled=True)
    picks = pltpu.with_memory_space_constraint(bands(band_start), pltpu.HBM)
    stacked, first, last = stack(
        got.reshape(owners * ROWS, LANES), picks, band_start, slowness.reshape(bins, samples), rows_y
    )
    low, high = exchange(first, last, "xline")
    before, after = exchange(*edges(stacked, low, high), "iline")
    return smooth(stacked, low, high, before, after, dip_shift.reshape(9, bins).T)


def solution(mesh):
    return jax.shard_map(
        body,
        mesh=mesh,
        in_specs=(
            P(AXES, None),
            P(AXES),
            P(AXES),
            P(AXES),
            P("xline", "iline", None),
            P(),
            P(None, "xline", "iline"),
        ),
        out_specs=P("xline", "iline", None),
        check_vma=False,
    )
```

```python
import functools

import jax
import jax.numpy as jnp
from jax import lax
from jax.experimental import pallas as pl
from jax.experimental.pallas import tpu as pltpu
from jax.sharding import PartitionSpec as P

BAND = 8
DIP = 4
REACH = BAND - 1
LANES = 128
CAP = 5
ROWS = 62
PARTS = 4
REACHED = 144
STEP = 32
HALVES = (0.5, 1.5, 2.5, 3.5)
VMEM = pl.BlockSpec(memory_space=pltpu.VMEM)
HBM = pl.BlockSpec(memory_space=pltpu.HBM)

CENTER_WEIGHT = 0.5
SIDE_WEIGHT = 0.0625

AXES = ("xline", "iline")
F32 = jnp.float32
BF16 = jnp.bfloat16


def iota(shape, dim):
    return lax.broadcasted_iota(jnp.int32, shape, dim)


def in_line(value):
    return jnp.concatenate([value[i : i + 1, :] for i in range(value.shape[0])], axis=1)


def dispatch_kernel(owners, traces_hbm, owner_hbm, cell_hbm, offset_hbm, out_ref, traces_ref, owner_ref, cell_ref, offset_ref, stage, packed, arrived, sent):
    pairs = ((owner_hbm, owner_ref), (cell_hbm, cell_ref), (offset_hbm, offset_ref), (traces_hbm, traces_ref))
    copies = [pltpu.make_async_copy(there, here, arrived.at[i]) for i, (there, here) in enumerate(pairs)]
    for copy in copies:
        copy.start()
    rows, samples = traces_ref.shape
    blocks = samples // LANES
    for copy in copies[:3]:
        copy.wait()
    owner = in_line(owner_ref[...])
    hot = (iota((owners, rows), 0) == owner).astype(F32)
    earlier = (iota((rows, rows), 0) < iota((rows, rows), 1)).astype(F32).astype(BF16)
    counts = jnp.dot(hot.astype(BF16), earlier, preferred_element_type=F32)
    rank = jnp.sum(hot * counts, axis=0, keepdims=True)
    picks = [jnp.where(rank == float(k), hot, 0.0).astype(BF16) for k in range(CAP)]
    pick = jnp.concatenate(picks, axis=0)
    meta = jnp.zeros((owners, LANES), F32)
    line = iota((LANES, rows), 0)
    offset = in_line(offset_ref[...].astype(F32))
    cell = in_line(cell_ref[...] + 1).astype(F32)
    for k in range(CAP):
        source = jnp.where(line == 8 * k, offset, jnp.where(line == 8 * k + 1, cell, 0.0))
        meta = meta + lax.dot_general(
            picks[k], source.astype(BF16), (((1,), (1,)), ((), ())), preferred_element_type=F32
        )
    stage[pl.ds(CAP * blocks, owners, stride=ROWS), :] = meta
    for row in range(CAP * blocks + 1, ROWS):
        stage[pl.ds(row, owners, stride=ROWS), :] = jnp.zeros((owners, LANES), F32)
    copies[3].wait()
    wrapped = iota((rows, LANES), 1) < REACH

    def turned(block):
        return pltpu.roll(traces_ref[:, block * LANES : (block + 1) * LANES], REACH, 1)

    previous = turned(blocks - 1)
    for tile in range(0, blocks, 2):
        one, two = turned(tile), turned(tile + 1)
        moved = jnp.concatenate([jnp.where(wrapped, previous, one), jnp.where(wrapped, one, two)], axis=1)
        previous = two
        placed = jnp.dot(pick, moved, preferred_element_type=F32)
        for k in range(CAP):
            for half in range(2):
                stage[pl.ds(k * blocks + tile + half, owners, stride=ROWS), :] = placed[
                    k * owners : (k + 1) * owners, half * LANES : (half + 1) * LANES
                ]
    size = owners * ROWS // PARTS
    sends = []
    for part in range(PARTS):
        here = pl.ds(part * size, size)
        packed[here, :] = stage[here, :].astype(BF16)
        sends.append(pltpu.make_async_copy(packed.at[here, :], out_ref.at[here, :], sent.at[part]))
        sends[-1].start()
    for copy in sends:
        copy.wait()


def dispatch(traces, owner, cell, offset, owners):
    rows, samples = traces.shape
    return pl.pallas_call(
        functools.partial(dispatch_kernel, owners),
        in_specs=[HBM] * 4,
        out_specs=HBM,
        out_shape=jax.ShapeDtypeStruct((owners * ROWS, LANES), BF16),
        scratch_shapes=[
            pltpu.VMEM((rows, samples), BF16),
            pltpu.VMEM((rows // LANES, LANES), jnp.int32),
            pltpu.VMEM((rows // LANES, LANES), jnp.int32),
            pltpu.VMEM((rows // LANES, LANES), BF16),
            pltpu.VMEM((owners * ROWS, LANES), F32),
            pltpu.VMEM((owners * ROWS, LANES), BF16),
            pltpu.SemaphoreType.DMA((4,)),
            pltpu.SemaphoreType.DMA((PARTS,)),
        ],
        name="dispatch",
    )(traces, *(v.reshape(rows // LANES, LANES) for v in (owner, cell, offset)))


def bands_kernel(start_ref, out_ref):
    first = start_ref[...] + (REACH - pl.program_id(0) * LANES)
    place = iota((REACHED, LANES), 0) - first
    for i, half in enumerate(HALVES):
        low = (place == int(3.5 - half)).astype(F32)
        high = (place == int(3.5 + half)).astype(F32)
        out_ref[0, :, i * LANES : (i + 1) * LANES] = (0.5 * (low + high)).astype(BF16)
        out_ref[0, :, (4 + i) * LANES : (5 + i) * LANES] = (half * (low - high)).astype(BF16)


def bands(band_start):
    samples = band_start.shape[0]
    blocks = samples // LANES
    return pl.pallas_call(
        bands_kernel,
        grid=(blocks,),
        in_specs=[pl.BlockSpec((1, LANES), lambda b: (0, b))],
        out_specs=pl.BlockSpec((1, REACHED, BAND * LANES), lambda b: (b, 0, 0)),
        out_shape=jax.ShapeDtypeStruct((blocks, REACHED, BAND * LANES), BF16),
        name="bands",
    )(band_start.reshape(1, samples))


def split3(value):
    high = value.astype(BF16)
    rest = value - high.astype(F32)
    middle = rest.astype(BF16)
    low = (rest - middle.astype(F32)).astype(BF16)
    return high, middle, low


def correct(lag, band):
    square = lag * lag
    num = odd = den = None
    for i, half in enumerate(HALVES):
        near = square + (1.0 + half * half)
        if half == 0.5:
            prod = near * near - square
        else:
            prod = (square + (2.0 - 2.0 * half * half)) * square + (1.0 + half * half) ** 2
        both = 1.0 / prod
        share = near * both
        part, tilt = band(i) * share, band(4 + i) * both
        num, odd, den = (part, tilt, share) if num is None else (num + part, odd + tilt, den + share)
    return (num + lag * odd) / den


def stack_kernel(got_ref, bands_hbm, start_ref, slow_ref, out_ref, first_ref, last_ref, stage, bands_ref, window, scaled, member, fold, lags, pairs0, pairs1, moved0, moved1, arrived):
    blocks = bands_hbm.shape[0]

    def fetch(block):
        return pltpu.make_async_copy(bands_hbm.at[block], bands_ref.at[block], arrived.at[block])

    for block in range(blocks):
        fetch(block).start()
    bins = slow_ref.shape[0]
    sources = got_ref.shape[0] // ROWS
    items = CAP * sources
    stage[...] = got_ref[...].astype(F32)
    meta = stage[pl.ds(CAP * blocks, sources, stride=ROWS), :]
    across = meta.T
    lane = iota((sources, LANES), 1)
    total = jnp.zeros((bins, 1), F32)
    for k in range(CAP):
        here = slice(k * sources, (k + 1) * sources)
        offset = meta[:, 8 * k : 8 * k + 1]
        cell = meta[:, 8 * k + 1 : 8 * k + 2] - 1.0
        square = offset * offset
        high = square.astype(BF16).astype(F32)
        part = jnp.where(lane < 3 * bins, high, square - high)
        keep = ((lane % bins).astype(F32) == cell) & (lane < 6 * bins)
        scaled[here, :] = jnp.where(keep, part, 0.0).astype(BF16)
        ones = (across[8 * k + 1 : 8 * k + 2, :] == (iota((bins, sources), 0) + 1).astype(F32)).astype(F32)
        total = total + jnp.sum(ones, axis=1, keepdims=True)
        member[:, here] = ones.astype(BF16)
    fold[...] = jnp.broadcast_to(jnp.maximum(total, 1.0), fold.shape)

    def gather(block):
        for k in range(CAP):
            rows = stage[pl.ds(k * blocks + block % blocks, sources, stride=ROWS), :]
            window[block, k * sources : (k + 1) * sources, :] = rows.astype(BF16)

    def lanes(block):
        return slice(block * LANES, (block + 1) * LANES)

    def shift(block):
        parts = list(split3(slow_ref[:, lanes(block)]))
        parts = [p.astype(F32) for p in parts + parts] + [jnp.zeros((LANES - 6 * bins, LANES), F32)]
        table = jnp.concatenate(parts, axis=0).astype(BF16)
        added = jnp.dot(scaled[...], table, preferred_element_type=F32)
        ticks = iota((1, LANES), 1) + block * LANES
        time = ticks.astype(F32)
        total = jnp.where(ticks == 0, 1e-30, time * time) + added
        lags[block] = (start_ref[:, lanes(block)].astype(F32) + 3.5) - total * lax.rsqrt(total)

    def multiply(block, pairs):
        wide = jnp.concatenate([window[block], window[block + 1]], axis=1)

        def pick(half):
            cols = slice(half * LANES, (half + 2) * LANES)
            rows = jnp.concatenate([bands_ref[block, :, cols], jnp.zeros((2 * LANES - REACHED, 2 * LANES), BF16)], axis=0)
            pairs[:, cols] = jnp.dot(wide, rows, preferred_element_type=F32)

        return [functools.partial(pick, half) for half in range(0, BAND, 2)]

    def weigh(block, pairs, moved):
        def chunk(row):
            here = slice(row, row + STEP)
            lag = lags[block, here, :]
            value = correct(lag, lambda i: pairs[here, i * LANES : (i + 1) * LANES])
            high = value.astype(BF16)
            moved[here, :] = high
            moved[items + row : items + row + STEP, :] = (value - high.astype(F32)).astype(BF16)

        return [functools.partial(chunk, row) for row in range(0, items, STEP)]

    def total_up(block, moved):
        sums = jnp.dot(member[...], moved[:items, :], preferred_element_type=F32) + jnp.dot(
            member[...], moved[items:, :], preferred_element_type=F32
        )
        out_ref[:, lanes(block)] = sums / fold[...]

    def interleave(few, many):
        for i, work in enumerate(many):
            for j, other in enumerate(few):
                if j * len(many) // len(few) == i:
                    other()
            work()

    gather(0)
    gather(1)
    for block in range(blocks):
        shift(block)
    for block in range(blocks):
        fetch(block).wait()
    pairs, moved = (pairs0, pairs1), (moved0, moved1)
    for work in multiply(0, pairs0):
        work()
    for block in range(blocks):
        now, later = block % 2, (block + 1) % 2
        ahead = []
        if block + 1 < blocks:
            gather(block + 2)
            ahead = multiply(block + 1, pairs[later])
        if block:
            total_up(block - 1, moved[later])
        interleave(ahead, weigh(block, pairs[now], moved[now]))
    total_up(blocks - 1, moved[(blocks - 1) % 2])
    first_ref[...] = out_ref[: first_ref.shape[0], :]
    last_ref[...] = out_ref[bins - last_ref.shape[0] :, :]


def stack(got, picks, band_start, slowness, rows_y):
    bins, samples = slowness.shape
    blocks = samples // LANES
    sources = got.shape[0] // ROWS
    items = CAP * sources
    edge = jax.ShapeDtypeStruct((rows_y, samples), F32)
    return pl.pallas_call(
        stack_kernel,
        in_specs=[VMEM, HBM, VMEM, VMEM],
        out_specs=[VMEM] * 3,
        out_shape=[jax.ShapeDtypeStruct((bins, samples), F32), edge, edge],
        scratch_shapes=[
            pltpu.VMEM((sources * ROWS, LANES), F32),
            pltpu.VMEM((blocks, REACHED, BAND * LANES), BF16),
            pltpu.VMEM((blocks + 1, items, LANES), BF16),
            pltpu.VMEM((items, LANES), BF16),
            pltpu.VMEM((bins, items), BF16),
            pltpu.VMEM((bins, LANES), F32),
            pltpu.VMEM((blocks, items, LANES), F32),
            pltpu.VMEM((items, BAND * LANES), F32),
            pltpu.VMEM((items, BAND * LANES), F32),
            pltpu.VMEM((2 * items, LANES), BF16),
            pltpu.VMEM((2 * items, LANES), BF16),
            pltpu.SemaphoreType.DMA((blocks,)),
        ],
        compiler_params=pltpu.CompilerParams(vmem_limit_bytes=40 << 20),
        name="stack",
    )(got, picks, band_start.reshape(1, samples), slowness)


def edges_kernel(stack_ref, low_ref, high_ref, first_ref, last_ref):
    height = low_ref.shape[0]
    width = stack_ref.shape[0] // height
    for y, ref in ((0, first_ref), (height - 1, last_ref)):
        ref[0:1, :] = low_ref[y : y + 1, :]
        for x in range(width):
            ref[x + 1 : x + 2, :] = stack_ref[x * height + y : x * height + y + 1, :]
        ref[width + 1 : width + 2, :] = high_ref[y : y + 1, :]


def edges(stacked, low, high):
    rows_y, samples = low.shape
    edge = jax.ShapeDtypeStruct((stacked.shape[0] // rows_y + 2, samples), F32)
    return pl.pallas_call(
        edges_kernel,
        in_specs=[VMEM] * 3,
        out_specs=[VMEM] * 2,
        out_shape=[edge, edge],
        compiler_params=pltpu.CompilerParams(vmem_limit_bytes=8 << 20),
        name="edges",
    )(stacked, low, high)


def inner_dip(dip, width, height):
    neighbour, bin_of = iota(dip.shape, 1), iota(dip.shape, 0)
    bin_x = lax.axis_index("xline") * width + bin_of // height + neighbour // 3 - 1
    bin_y = lax.axis_index("iline") * height + bin_of % height + neighbour % 3 - 1
    limit_x, limit_y = lax.axis_size("xline") * width, lax.axis_size("iline") * height
    inside = (bin_x >= 0) & (bin_x < limit_x) & (bin_y >= 0) & (bin_y < limit_y)
    return jnp.where(inside, dip, 2 * DIP + 1)


def steer(terms):
    shape = terms[0][0].shape
    samples = shape[1]
    time = iota(shape, 1)
    result = None
    for lag in range(-DIP, DIP + 1):
        part = None
        for rows, dip, factor in terms:
            value = jnp.where(dip == lag, factor, 0.0) * rows
            part = value if part is None else part + value
        if lag:
            part = pltpu.roll(part, (-lag) % samples, 1)
            part = jnp.where((time + lag >= 0) & (time + lag < samples), part, 0.0)
        result = part if result is None else result + part
    return result


def factor_of(n):
    return CENTER_WEIGHT if n == 4 else SIDE_WEIGHT


def smooth_kernel(stack_ref, low_ref, high_ref, dip_ref, out_ref, padded):
    height = low_ref.shape[0]
    bins, samples = stack_ref.shape
    width = bins // height
    pitch = height + 2
    zero = jnp.zeros((1, samples), F32)
    for x in range(width + 2):
        row = x * pitch
        padded[row : row + 1, :] = zero
        if x == 0:
            inner = low_ref[...]
        elif x == width + 1:
            inner = high_ref[...]
        else:
            inner = stack_ref[(x - 1) * height : x * height, :]
        padded[row + 1 : row + 1 + height, :] = inner
        padded[row + 1 + height : row + pitch, :] = zero
    dip = inner_dip(dip_ref[...], width, height)
    terms = []
    for n in range(9):
        dx, dy = n // 3, n % 3
        rows = [(dx + x) * pitch + dy for x in range(width)]
        near = jnp.concatenate([padded[r : r + height, :] for r in rows], axis=0)
        terms.append((near, dip[:, n : n + 1], factor_of(n)))
    out_ref[...] = steer(terms)


def border_kernel(part_ref, before_ref, after_ref, dip_ref, out_ref):
    width = before_ref.shape[0] - 2
    bins, samples = part_ref.shape
    height = bins // width
    dip = inner_dip(dip_ref[...], width, height)
    terms = []
    for dx in range(3):
        near = jnp.concatenate([before_ref[dx : dx + width, :], after_ref[dx : dx + width, :]], axis=0)
        shifts = [dip[x * height : x * height + 1, 3 * dx : 3 * dx + 1] for x in range(width)]
        shifts += [dip[(x + 1) * height - 1 : (x + 1) * height, 3 * dx + 2 : 3 * dx + 3] for x in range(width)]
        terms.append((near, jnp.concatenate(shifts, axis=0), SIDE_WEIGHT))
    border = steer(terms)
    for x in range(width):
        out_ref[x] = part_ref[x * height : (x + 1) * height, :]
        out_ref[x, 0:1, :] = part_ref[x * height : x * height + 1, :] + border[x : x + 1, :]
        last = (x + 1) * height - 1
        out_ref[x, height - 1 : height, :] = part_ref[last : last + 1, :] + border[width + x : width + x + 1, :]


def smooth(stacked, low, high, dip):
    rows_y, samples = low.shape
    bins = stacked.shape[0]
    rows_x = bins // rows_y
    return pl.pallas_call(
        smooth_kernel,
        in_specs=[VMEM] * 4,
        out_specs=VMEM,
        out_shape=jax.ShapeDtypeStruct((bins, samples), F32),
        scratch_shapes=[pltpu.VMEM(((rows_x + 2) * (rows_y + 2), samples), F32)],
        compiler_params=pltpu.CompilerParams(vmem_limit_bytes=8 << 20),
        name="smooth",
    )(stacked, low, high, dip)


def border(part, before, after, dip):
    bins, samples = part.shape
    rows_x = before.shape[0] - 2
    return pl.pallas_call(
        border_kernel,
        in_specs=[VMEM] * 4,
        out_specs=VMEM,
        out_shape=jax.ShapeDtypeStruct((rows_x, bins // rows_x, samples), F32),
        compiler_params=pltpu.CompilerParams(vmem_limit_bytes=8 << 20),
        name="border",
    )(part, before, after, dip)


def exchange(first, last, axis):
    size = lax.axis_size(axis)
    before = lax.ppermute(last, axis, [(i, (i + 1) % size) for i in range(size)])
    after = lax.ppermute(first, axis, [((i + 1) % size, i) for i in range(size)])
    return before, after


def body(traces, trace_offset, trace_owner, trace_cell, slowness, band_start, dip_shift):
    owners = lax.axis_size(AXES)
    rows_x, rows_y, samples = slowness.shape
    bins = rows_x * rows_y
    send = dispatch(traces, trace_owner, trace_cell, trace_offset, owners)
    send = send.reshape(owners, ROWS // 2, 2, LANES)
    got = lax.all_to_all(send, AXES, split_axis=0, concat_axis=0, tiled=True)
    picks = pltpu.with_memory_space_constraint(bands(band_start), pltpu.HBM)
    stacked, first, last = stack(
        got.reshape(owners * ROWS, LANES), picks, band_start, slowness.reshape(bins, samples), rows_y
    )
    low, high = exchange(first, last, "xline")
    before, after = exchange(*edges(stacked, low, high), "iline")
    dip = dip_shift.reshape(9, bins).T
    return border(smooth(stacked, low, high, dip), before, after, dip)


def solution(mesh):
    return jax.shard_map(
        body,
        mesh=mesh,
        in_specs=(
            P(AXES, None),
            P(AXES),
            P(AXES),
            P(AXES),
            P("xline", "iline", None),
            P(),
            P(None, "xline", "iline"),
        ),
        out_specs=P("xline", "iline", None),
        check_vma=False,
    )
```

```python
import functools

import jax
import jax.numpy as jnp
from jax import lax
from jax.experimental import pallas as pl
from jax.experimental.pallas import tpu as pltpu
from jax.sharding import PartitionSpec as P

BAND = 8
DIP = 4
REACH = BAND - 1
LANES = 128
CAP = 5
ROWS = 62
REACHED = 144
DISPATCH_LIMIT = 24
STEP = 32
HALVES = (0.5, 1.5, 2.5, 3.5)
VMEM = pl.BlockSpec(memory_space=pltpu.VMEM)
HBM = pl.BlockSpec(memory_space=pltpu.HBM)

CENTER_WEIGHT = 0.5
SIDE_WEIGHT = 0.0625

AXES = ("xline", "iline")
F32 = jnp.float32
BF16 = jnp.bfloat16


def iota(shape, dim):
    return lax.broadcasted_iota(jnp.int32, shape, dim)


def in_line(value):
    return jnp.concatenate([value[i : i + 1, :] for i in range(value.shape[0])], axis=1)


def dispatch_kernel(owners, traces_hbm, owner_hbm, cell_hbm, offset_hbm, out_ref, traces_ref, owner_ref, cell_ref, offset_ref, stage, arrived):
    pairs = ((owner_hbm, owner_ref), (cell_hbm, cell_ref), (offset_hbm, offset_ref), (traces_hbm, traces_ref))
    copies = [pltpu.make_async_copy(there, here, arrived.at[i]) for i, (there, here) in enumerate(pairs)]
    for copy in copies:
        copy.start()
    rows, samples = traces_ref.shape
    blocks = samples // LANES
    for copy in copies[:3]:
        copy.wait()
    owner = in_line(owner_ref[...])
    hot = (iota((owners, rows), 0) == owner).astype(F32)
    earlier = (iota((rows, rows), 0) < iota((rows, rows), 1)).astype(F32).astype(BF16)
    counts = jnp.dot(hot.astype(BF16), earlier, preferred_element_type=F32)
    rank = jnp.sum(hot * counts, axis=0, keepdims=True)
    picks = [jnp.where(rank == float(k), hot, 0.0).astype(BF16) for k in range(CAP)]
    pick = jnp.concatenate(picks, axis=0)
    meta = jnp.zeros((owners, LANES), F32)
    line = iota((LANES, rows), 0)
    offset = in_line(offset_ref[...].astype(F32))
    cell = in_line(cell_ref[...] + 1).astype(F32)
    for k in range(CAP):
        source = jnp.where(line == 8 * k, offset, jnp.where(line == 8 * k + 1, cell, 0.0))
        meta = meta + lax.dot_general(
            picks[k], source.astype(BF16), (((1,), (1,)), ((), ())), preferred_element_type=F32
        )
    stage[pl.ds(CAP * blocks, owners, stride=ROWS), :] = meta
    for row in range(CAP * blocks + 1, ROWS):
        stage[pl.ds(row, owners, stride=ROWS), :] = jnp.zeros((owners, LANES), F32)
    copies[3].wait()
    wrapped = iota((rows, LANES), 1) < REACH

    def turned(block):
        return pltpu.roll(traces_ref[:, block * LANES : (block + 1) * LANES], REACH, 1)

    previous = turned(blocks - 1)
    for tile in range(0, blocks, 2):
        one, two = turned(tile), turned(tile + 1)
        moved = jnp.concatenate([jnp.where(wrapped, previous, one), jnp.where(wrapped, one, two)], axis=1)
        previous = two
        placed = jnp.dot(pick, moved, preferred_element_type=F32)
        for k in range(CAP):
            for half in range(2):
                stage[pl.ds(k * blocks + tile + half, owners, stride=ROWS), :] = placed[
                    k * owners : (k + 1) * owners, half * LANES : (half + 1) * LANES
                ]
    out_ref[...] = stage[...].astype(BF16)


def dispatch(traces, owner, cell, offset, owners):
    rows, samples = traces.shape
    given = [traces] + [v.reshape(rows // LANES, LANES) for v in (owner, cell, offset)]
    return pl.pallas_call(
        functools.partial(dispatch_kernel, owners),
        in_specs=[HBM] * 4,
        out_specs=VMEM,
        out_shape=jax.ShapeDtypeStruct((owners * ROWS, LANES), BF16),
        scratch_shapes=[
            pltpu.VMEM((rows, samples), BF16),
            pltpu.VMEM((rows // LANES, LANES), jnp.int32),
            pltpu.VMEM((rows // LANES, LANES), jnp.int32),
            pltpu.VMEM((rows // LANES, LANES), BF16),
            pltpu.VMEM((owners * ROWS, LANES), F32),
            pltpu.SemaphoreType.DMA((4,)),
        ],
        compiler_params=pltpu.CompilerParams(vmem_limit_bytes=DISPATCH_LIMIT << 20),
        name="dispatch",
    )(*(pltpu.with_memory_space_constraint(v, pltpu.HBM) for v in given))


def split3(value):
    high = value.astype(BF16)
    rest = value - high.astype(F32)
    middle = rest.astype(BF16)
    low = (rest - middle.astype(F32)).astype(BF16)
    return high, middle, low


def correct(lag, band):
    square = lag * lag
    num = odd = den = None
    for i, half in enumerate(HALVES):
        near = square + (1.0 + half * half)
        if half == 0.5:
            prod = near * near - square
        else:
            prod = (square + (2.0 - 2.0 * half * half)) * square + (1.0 + half * half) ** 2
        both = 1.0 / prod
        share = near * both
        part, tilt = band(2 * i) * share, band(2 * i + 1) * both
        num, odd, den = (part, tilt, share) if num is None else (num + part, odd + tilt, den + share)
    return (num + lag * odd) / den


def stack_kernel(got_ref, start_ref, slow_ref, out_ref, first_ref, last_ref, stage, window, scaled, member, fold, lags, pairs0, pairs1, moved0, moved1):
    blocks = start_ref.shape[0]
    bins = slow_ref.shape[0] * slow_ref.shape[1]
    sources = got_ref.shape[0] // ROWS
    items = CAP * sources
    stage[...] = got_ref[...].astype(F32)
    meta = stage[pl.ds(CAP * blocks, sources, stride=ROWS), :]
    across = meta.T
    lane = iota((sources, LANES), 1)
    total = jnp.zeros((bins, 1), F32)
    for k in range(CAP):
        here = slice(k * sources, (k + 1) * sources)
        offset = meta[:, 8 * k : 8 * k + 1]
        cell = meta[:, 8 * k + 1 : 8 * k + 2] - 1.0
        square = offset * offset
        high = square.astype(BF16).astype(F32)
        part = jnp.where(lane < 3 * bins, high, square - high)
        keep = ((lane % bins).astype(F32) == cell) & (lane < 6 * bins)
        scaled[here, :] = jnp.where(keep, part, 0.0).astype(BF16)
        ones = (across[8 * k + 1 : 8 * k + 2, :] == (iota((bins, sources), 0) + 1).astype(F32)).astype(F32)
        total = total + jnp.sum(ones, axis=1, keepdims=True)
        member[:, here] = ones.astype(BF16)
    fold[...] = jnp.broadcast_to(jnp.maximum(total, 1.0), fold.shape)

    def gather(block):
        for k in range(CAP):
            rows = stage[pl.ds(k * blocks + block % blocks, sources, stride=ROWS), :]
            window[block, k * sources : (k + 1) * sources, :] = rows.astype(BF16)

    def lanes(block):
        return slice(block * LANES, (block + 1) * LANES)

    def shift(block):
        parts = list(split3(jnp.concatenate([slow_ref[x, :, lanes(block)] for x in range(slow_ref.shape[0])], axis=0)))
        parts = [p.astype(F32) for p in parts + parts] + [jnp.zeros((LANES - 6 * bins, LANES), F32)]
        table = jnp.concatenate(parts, axis=0).astype(BF16)
        added = jnp.dot(scaled[...], table, preferred_element_type=F32)
        ticks = iota((1, LANES), 1) + block * LANES
        time = ticks.astype(F32)
        total = jnp.where(ticks == 0, 1e-30, time * time) + added
        lags[block] = (start_ref[block : block + 1, :].astype(F32) + 3.5) - total * lax.rsqrt(total)

    def multiply(block, pairs):
        wide = jnp.concatenate([window[block], window[block + 1]], axis=1)
        first = start_ref[block : block + 1, :] + (REACH - block * LANES)
        place = (iota((REACHED, LANES), 0) - first).astype(F32) - 3.5
        back, apart = (-place).astype(BF16), jnp.abs(place).astype(BF16)
        none = jnp.zeros((REACHED, LANES), BF16)

        def pick(i):
            chosen = apart == jnp.asarray(HALVES[i], BF16)
            rows = jnp.concatenate([jnp.where(chosen, jnp.asarray(0.5, BF16), none), jnp.where(chosen, back, none)], axis=1)
            rows = jnp.concatenate([rows, jnp.zeros((2 * LANES - REACHED, 2 * LANES), BF16)], axis=0)
            pairs[:, 2 * i * LANES : 2 * (i + 1) * LANES] = jnp.dot(wide, rows, preferred_element_type=F32)

        return [functools.partial(pick, i) for i in range(BAND // 2)]

    def weigh(block, pairs, moved):
        def chunk(row):
            here = slice(row, row + STEP)
            lag = lags[block, here, :]
            value = correct(lag, lambda i: pairs[here, i * LANES : (i + 1) * LANES])
            high = value.astype(BF16)
            moved[here, :] = high
            moved[items + row : items + row + STEP, :] = (value - high.astype(F32)).astype(BF16)

        return [functools.partial(chunk, row) for row in range(0, items, STEP)]

    def total_up(block, moved):
        sums = jnp.dot(member[...], moved[:items, :], preferred_element_type=F32) + jnp.dot(
            member[...], moved[items:, :], preferred_element_type=F32
        )
        out_ref[:, lanes(block)] = sums / fold[...]

    def interleave(few, many):
        for i, work in enumerate(many):
            for j, other in enumerate(few):
                if j * len(many) // len(few) == i:
                    other()
            work()

    gather(0)
    gather(1)
    for block in range(blocks):
        shift(block)
    pairs, moved = (pairs0, pairs1), (moved0, moved1)
    for work in multiply(0, pairs0):
        work()
    for block in range(blocks):
        now, later = block % 2, (block + 1) % 2
        ahead = []
        if block + 1 < blocks:
            gather(block + 2)
            ahead = multiply(block + 1, pairs[later])
        if block:
            total_up(block - 1, moved[later])
        interleave(ahead, weigh(block, pairs[now], moved[now]))
    total_up(blocks - 1, moved[(blocks - 1) % 2])
    first_ref[...] = out_ref[: first_ref.shape[0], :]
    last_ref[...] = out_ref[bins - last_ref.shape[0] :, :]


def stack(got, band_start, slowness):
    rows_x, rows_y, samples = slowness.shape
    bins = rows_x * rows_y
    blocks = samples // LANES
    sources = got.shape[0] // ROWS
    items = CAP * sources
    edge = jax.ShapeDtypeStruct((rows_y, samples), F32)
    return pl.pallas_call(
        stack_kernel,
        in_specs=[VMEM] * 3,
        out_specs=[VMEM] * 3,
        out_shape=[jax.ShapeDtypeStruct((bins, samples), F32), edge, edge],
        scratch_shapes=[
            pltpu.VMEM((sources * ROWS, LANES), F32),
            pltpu.VMEM((blocks + 1, items, LANES), BF16),
            pltpu.VMEM((items, LANES), BF16),
            pltpu.VMEM((bins, items), BF16),
            pltpu.VMEM((bins, LANES), F32),
            pltpu.VMEM((blocks, items, LANES), F32),
            pltpu.VMEM((items, BAND * LANES), F32),
            pltpu.VMEM((items, BAND * LANES), F32),
            pltpu.VMEM((2 * items, LANES), BF16),
            pltpu.VMEM((2 * items, LANES), BF16),
        ],
        compiler_params=pltpu.CompilerParams(vmem_limit_bytes=40 << 20),
        name="stack",
    )(got, band_start.reshape(blocks, LANES), slowness)


def edges_kernel(stack_ref, low_ref, high_ref, first_ref, last_ref):
    height = low_ref.shape[0]
    width = stack_ref.shape[0] // height
    for y, ref in ((0, first_ref), (height - 1, last_ref)):
        ref[0:1, :] = low_ref[y : y + 1, :]
        for x in range(width):
            ref[x + 1 : x + 2, :] = stack_ref[x * height + y : x * height + y + 1, :]
        ref[width + 1 : width + 2, :] = high_ref[y : y + 1, :]


def edges(stacked, low, high):
    rows_y, samples = low.shape
    edge = jax.ShapeDtypeStruct((stacked.shape[0] // rows_y + 2, samples), F32)
    return pl.pallas_call(
        edges_kernel,
        in_specs=[VMEM] * 3,
        out_specs=[VMEM] * 2,
        out_shape=[edge, edge],
        compiler_params=pltpu.CompilerParams(vmem_limit_bytes=8 << 20),
        name="edges",
    )(stacked, low, high)


def inner_dip(dip, width, height):
    neighbour, bin_of = iota(dip.shape, 1), iota(dip.shape, 0)
    bin_x = lax.axis_index("xline") * width + bin_of // height + neighbour // 3 - 1
    bin_y = lax.axis_index("iline") * height + bin_of % height + neighbour % 3 - 1
    limit_x, limit_y = lax.axis_size("xline") * width, lax.axis_size("iline") * height
    inside = (bin_x >= 0) & (bin_x < limit_x) & (bin_y >= 0) & (bin_y < limit_y)
    return jnp.where(inside, dip, 2 * DIP + 1)


def steer(terms):
    shape = terms[0][0].shape
    samples = shape[1]
    time = iota(shape, 1)
    result = None
    for lag in range(-DIP, DIP + 1):
        part = None
        for rows, dip, factor in terms:
            value = jnp.where(dip == lag, factor, 0.0) * rows
            part = value if part is None else part + value
        if lag:
            part = pltpu.roll(part, (-lag) % samples, 1)
            part = jnp.where((time + lag >= 0) & (time + lag < samples), part, 0.0)
        result = part if result is None else result + part
    return result


def factor_of(n):
    return CENTER_WEIGHT if n == 4 else SIDE_WEIGHT


def smooth_kernel(stack_ref, low_ref, high_ref, dip_ref, out_ref, padded):
    height = low_ref.shape[0]
    bins, samples = stack_ref.shape
    width = bins // height
    pitch = height + 2
    zero = jnp.zeros((1, samples), F32)
    for x in range(width + 2):
        row = x * pitch
        padded[row : row + 1, :] = zero
        if x == 0:
            inner = low_ref[...]
        elif x == width + 1:
            inner = high_ref[...]
        else:
            inner = stack_ref[(x - 1) * height : x * height, :]
        padded[row + 1 : row + 1 + height, :] = inner
        padded[row + 1 + height : row + pitch, :] = zero
    dip = inner_dip(dip_ref[...], width, height)
    terms = []
    for n in range(9):
        dx, dy = n // 3, n % 3
        rows = [(dx + x) * pitch + dy for x in range(width)]
        near = jnp.concatenate([padded[r : r + height, :] for r in rows], axis=0)
        terms.append((near, dip[:, n : n + 1], factor_of(n)))
    out_ref[...] = steer(terms)


def border_kernel(part_ref, before_ref, after_ref, dip_ref, out_ref):
    width = before_ref.shape[0] - 2
    bins, samples = part_ref.shape
    height = bins // width
    dip = inner_dip(dip_ref[...], width, height)
    terms = []
    for dx in range(3):
        near = jnp.concatenate([before_ref[dx : dx + width, :], after_ref[dx : dx + width, :]], axis=0)
        shifts = [dip[x * height : x * height + 1, 3 * dx : 3 * dx + 1] for x in range(width)]
        shifts += [dip[(x + 1) * height - 1 : (x + 1) * height, 3 * dx + 2 : 3 * dx + 3] for x in range(width)]
        terms.append((near, jnp.concatenate(shifts, axis=0), SIDE_WEIGHT))
    border = steer(terms)
    for x in range(width):
        out_ref[x] = part_ref[x * height : (x + 1) * height, :]
        out_ref[x, 0:1, :] = part_ref[x * height : x * height + 1, :] + border[x : x + 1, :]
        last = (x + 1) * height - 1
        out_ref[x, height - 1 : height, :] = part_ref[last : last + 1, :] + border[width + x : width + x + 1, :]


def smooth(stacked, low, high, dip):
    rows_y, samples = low.shape
    bins = stacked.shape[0]
    rows_x = bins // rows_y
    return pl.pallas_call(
        smooth_kernel,
        in_specs=[VMEM] * 4,
        out_specs=VMEM,
        out_shape=jax.ShapeDtypeStruct((bins, samples), F32),
        scratch_shapes=[pltpu.VMEM(((rows_x + 2) * (rows_y + 2), samples), F32)],
        compiler_params=pltpu.CompilerParams(vmem_limit_bytes=8 << 20),
        name="smooth",
    )(stacked, low, high, dip)


def border(part, before, after, dip):
    bins, samples = part.shape
    rows_x = before.shape[0] - 2
    return pl.pallas_call(
        border_kernel,
        in_specs=[VMEM] * 4,
        out_specs=VMEM,
        out_shape=jax.ShapeDtypeStruct((rows_x, bins // rows_x, samples), F32),
        compiler_params=pltpu.CompilerParams(vmem_limit_bytes=8 << 20),
        name="border",
    )(part, before, after, dip)


def exchange(first, last, axis):
    size = lax.axis_size(axis)
    before = lax.ppermute(last, axis, [(i, (i + 1) % size) for i in range(size)])
    after = lax.ppermute(first, axis, [((i + 1) % size, i) for i in range(size)])
    return before, after


def body(traces, trace_offset, trace_owner, trace_cell, slowness, band_start, dip_shift):
    owners = lax.axis_size(AXES)
    rows_x, rows_y, samples = slowness.shape
    bins = rows_x * rows_y
    send = dispatch(traces, trace_owner, trace_cell, trace_offset, owners)
    send = send.reshape(owners, ROWS // 2, 2, LANES)
    got = lax.all_to_all(send, AXES, split_axis=0, concat_axis=0, tiled=True)
    stacked, first, last = stack(got.reshape(owners * ROWS, LANES), band_start, slowness)
    low, high = exchange(first, last, "xline")
    before, after = exchange(*edges(stacked, low, high), "iline")
    dip = dip_shift.reshape(9, bins).T
    return border(smooth(stacked, low, high, dip), before, after, dip)


def solution(mesh):
    return jax.shard_map(
        body,
        mesh=mesh,
        in_specs=(
            P(AXES, None),
            P(AXES),
            P(AXES),
            P(AXES),
            P("xline", "iline", None),
            P(),
            P(None, "xline", "iline"),
        ),
        out_specs=P("xline", "iline", None),
        check_vma=False,
    )
```

```python
import functools

import jax
import jax.numpy as jnp
from jax import lax
from jax.experimental import pallas as pl
from jax.experimental.pallas import tpu as pltpu
from jax.sharding import PartitionSpec as P

BAND = 8
DIP = 4
REACH = BAND - 1
LANES = 128
CAP = 5
ROWS = 62
REACHED = 144
PARTS = 2
DISPATCH_LIMIT = 24
STEP = 32
HALVES = (0.5, 1.5, 2.5, 3.5)
VMEM = pl.BlockSpec(memory_space=pltpu.VMEM)
HBM = pl.BlockSpec(memory_space=pltpu.HBM)

CENTER_WEIGHT = 0.5
SIDE_WEIGHT = 0.0625

AXES = ("xline", "iline")
F32 = jnp.float32
BF16 = jnp.bfloat16


def iota(shape, dim):
    return lax.broadcasted_iota(jnp.int32, shape, dim)


def in_line(value):
    return jnp.concatenate([value[i : i + 1, :] for i in range(value.shape[0])], axis=1)


def dispatch_kernel(owners, traces_hbm, owner_hbm, cell_hbm, offset_hbm, out_ref, traces_ref, owner_ref, cell_ref, offset_ref, rolled, stage, arrived):
    pairs = ((owner_hbm, owner_ref), (cell_hbm, cell_ref), (offset_hbm, offset_ref), (traces_hbm, traces_ref))
    copies = [pltpu.make_async_copy(there, here, arrived.at[i]) for i, (there, here) in enumerate(pairs)]
    for copy in copies:
        copy.start()
    rows, samples = traces_ref.shape
    blocks = samples // LANES
    for copy in copies[:3]:
        copy.wait()
    owner = in_line(owner_ref[...])
    hot = (iota((owners, rows), 0) == owner).astype(F32)
    earlier = (iota((rows, rows), 0) < iota((rows, rows), 1)).astype(F32).astype(BF16)
    counts = jnp.dot(hot.astype(BF16), earlier, preferred_element_type=F32)
    rank = jnp.sum(hot * counts, axis=0, keepdims=True)
    picks = [jnp.where(rank == float(k), hot, 0.0).astype(BF16) for k in range(CAP)]
    meta = jnp.zeros((owners, LANES), F32)
    line = iota((LANES, rows), 0)
    offset = in_line(offset_ref[...].astype(F32))
    cell = in_line(cell_ref[...] + 1).astype(F32)
    for k in range(CAP):
        source = jnp.where(line == 8 * k, offset, jnp.where(line == 8 * k + 1, cell, 0.0))
        meta = meta + lax.dot_general(
            picks[k], source.astype(BF16), (((1,), (1,)), ((), ())), preferred_element_type=F32
        )
    stage[pl.ds(CAP * blocks, owners, stride=ROWS), :] = meta
    for row in range(CAP * blocks + 1, ROWS):
        stage[pl.ds(row, owners, stride=ROWS), :] = jnp.zeros((owners, LANES), F32)
    copies[3].wait()
    wrapped = iota((rows, LANES), 1) < REACH

    def turned(block):
        return pltpu.roll(traces_ref[:, block * LANES : (block + 1) * LANES], REACH, 1)

    previous = turned(blocks - 1)
    for block in range(blocks):
        here = turned(block)
        rolled[:, block * LANES : (block + 1) * LANES] = jnp.where(wrapped, previous, here)
        previous = here
    part = owners // PARTS
    for low in range(0, owners, part):
        pick = jnp.concatenate([picks[k][low : low + part, :] for k in range(CAP)], axis=0)
        for tile in range(0, blocks, 2):
            placed = jnp.dot(pick, rolled[:, tile * LANES : (tile + 2) * LANES], preferred_element_type=F32)
            for k in range(CAP):
                for half in range(2):
                    stage[pl.ds(low * ROWS + k * blocks + tile + half, part, stride=ROWS), :] = placed[
                        k * part : (k + 1) * part, half * LANES : (half + 1) * LANES
                    ]
        here = slice(low * ROWS, (low + part) * ROWS)
        out_ref[here, :] = stage[here, :].astype(BF16)


def dispatch(traces, owner, cell, offset, owners):
    rows, samples = traces.shape
    given = [traces] + [v.reshape(rows // LANES, LANES) for v in (owner, cell, offset)]
    return pl.pallas_call(
        functools.partial(dispatch_kernel, owners),
        in_specs=[HBM] * 4,
        out_specs=VMEM,
        out_shape=jax.ShapeDtypeStruct((owners * ROWS, LANES), BF16),
        scratch_shapes=[
            pltpu.VMEM((rows, samples), BF16),
            pltpu.VMEM((rows // LANES, LANES), jnp.int32),
            pltpu.VMEM((rows // LANES, LANES), jnp.int32),
            pltpu.VMEM((rows // LANES, LANES), BF16),
            pltpu.VMEM((rows, samples), BF16),
            pltpu.VMEM((owners * ROWS, LANES), F32),
            pltpu.SemaphoreType.DMA((4,)),
        ],
        compiler_params=pltpu.CompilerParams(vmem_limit_bytes=DISPATCH_LIMIT << 20),
        name="dispatch",
    )(*(pltpu.with_memory_space_constraint(v, pltpu.HBM) for v in given))


def split3(value):
    high = value.astype(BF16)
    rest = value - high.astype(F32)
    middle = rest.astype(BF16)
    low = (rest - middle.astype(F32)).astype(BF16)
    return high, middle, low


def correct(lag, band):
    square = lag * lag
    num = odd = den = None
    for i, half in enumerate(HALVES):
        near = square + (1.0 + half * half)
        if half == 0.5:
            prod = near * near - square
        else:
            prod = (square + (2.0 - 2.0 * half * half)) * square + (1.0 + half * half) ** 2
        both = 1.0 / prod
        share = near * both
        part, tilt = band(2 * i) * share, band(2 * i + 1) * both
        num, odd, den = (part, tilt, share) if num is None else (num + part, odd + tilt, den + share)
    return (num + lag * odd) / den


def stack_kernel(got_ref, start_ref, slow_ref, out_ref, first_ref, last_ref, stage, window, scaled, member, fold, lags, pairs0, pairs1, moved0, moved1):
    blocks = start_ref.shape[0]
    bins = slow_ref.shape[0] * slow_ref.shape[1]
    sources = got_ref.shape[0] // ROWS
    items = CAP * sources
    stage[...] = got_ref[...].astype(F32)
    meta = stage[pl.ds(CAP * blocks, sources, stride=ROWS), :]
    across = meta.T
    lane = iota((sources, LANES), 1)
    total = jnp.zeros((bins, 1), F32)
    for k in range(CAP):
        here = slice(k * sources, (k + 1) * sources)
        offset = meta[:, 8 * k : 8 * k + 1]
        cell = meta[:, 8 * k + 1 : 8 * k + 2] - 1.0
        square = offset * offset
        high = square.astype(BF16).astype(F32)
        part = jnp.where(lane < 3 * bins, high, square - high)
        keep = ((lane % bins).astype(F32) == cell) & (lane < 6 * bins)
        ones = (lane >= 6 * bins) & (lane < 6 * bins + 3)
        scaled[here, :] = jnp.where(keep, part, jnp.where(ones, 1.0, 0.0)).astype(BF16)
        ones = (across[8 * k + 1 : 8 * k + 2, :] == (iota((bins, sources), 0) + 1).astype(F32)).astype(F32)
        total = total + jnp.sum(ones, axis=1, keepdims=True)
        member[:, here] = ones.astype(BF16)
    fold[...] = jnp.broadcast_to(jnp.maximum(total, 1.0), fold.shape)

    def gather(block):
        for k in range(CAP):
            rows = stage[pl.ds(k * blocks + block % blocks, sources, stride=ROWS), :]
            window[block, k * sources : (k + 1) * sources, :] = rows.astype(BF16)

    def lanes(block):
        return slice(block * LANES, (block + 1) * LANES)

    def shift(block):
        parts = list(split3(jnp.concatenate([slow_ref[x, :, lanes(block)] for x in range(slow_ref.shape[0])], axis=0)))
        ticks = iota((bins, LANES), 1) + block * LANES
        time = ticks.astype(F32)
        squares = split3(jnp.where(ticks == 0, 1e-30, time * time))
        line = iota((bins, LANES), 0)
        clock = jnp.zeros((bins, LANES), F32)
        for i, part in enumerate(squares):
            clock = jnp.where(line == i, part.astype(F32), clock)
        parts = [p.astype(F32) for p in parts + parts] + [clock, jnp.zeros((LANES - 7 * bins, LANES), F32)]
        total = jnp.dot(scaled[...], jnp.concatenate(parts, axis=0).astype(BF16), preferred_element_type=F32)
        lags[block % 3] = (start_ref[block : block + 1, :].astype(F32) + 3.5) - total * lax.rsqrt(total)

    def multiply(block, pairs):
        wide = jnp.concatenate([window[block], window[block + 1]], axis=1)
        first = start_ref[block : block + 1, :] + (REACH - block * LANES)
        place = (iota((REACHED, LANES), 0) - first).astype(F32) - 3.5
        back, apart = (-place).astype(BF16), jnp.abs(place).astype(BF16)
        none = jnp.zeros((REACHED, LANES), BF16)

        def pick(i):
            chosen = apart == jnp.asarray(HALVES[i], BF16)
            rows = jnp.concatenate([jnp.where(chosen, jnp.asarray(0.5, BF16), none), jnp.where(chosen, back, none)], axis=1)
            rows = jnp.concatenate([rows, jnp.zeros((2 * LANES - REACHED, 2 * LANES), BF16)], axis=0)
            pairs[:, 2 * i * LANES : 2 * (i + 1) * LANES] = jnp.dot(wide, rows, preferred_element_type=F32)

        return [functools.partial(pick, i) for i in range(BAND // 2)]

    def weigh(block, pairs, moved):
        def chunk(row):
            here = slice(row, row + STEP)
            lag = lags[block % 3, here, :]
            value = correct(lag, lambda i: pairs[here, i * LANES : (i + 1) * LANES])
            high = value.astype(BF16)
            moved[here, :] = high
            moved[items + row : items + row + STEP, :] = (value - high.astype(F32)).astype(BF16)

        return [functools.partial(chunk, row) for row in range(0, items, STEP)]

    def total_up(block, moved):
        sums = jnp.dot(member[...], moved[:items, :], preferred_element_type=F32) + jnp.dot(
            member[...], moved[items:, :], preferred_element_type=F32
        )
        out_ref[:, lanes(block)] = sums / fold[...]

    def interleave(few, many):
        for i, work in enumerate(many):
            for j, other in enumerate(few):
                if j * len(many) // len(few) == i:
                    other()
            work()

    gather(0)
    gather(1)
    shift(0)
    shift(1)
    pairs, moved = (pairs0, pairs1), (moved0, moved1)
    for work in multiply(0, pairs0):
        work()
    for block in range(blocks):
        now, later = block % 2, (block + 1) % 2
        ahead = []
        if block + 1 < blocks:
            gather(block + 2)
            if block + 2 < blocks:
                shift(block + 2)
            ahead = multiply(block + 1, pairs[later])
        if block:
            total_up(block - 1, moved[later])
        interleave(ahead, weigh(block, pairs[now], moved[now]))
    total_up(blocks - 1, moved[(blocks - 1) % 2])
    first_ref[...] = out_ref[: first_ref.shape[0], :]
    last_ref[...] = out_ref[bins - last_ref.shape[0] :, :]


def stack(got, band_start, slowness):
    rows_x, rows_y, samples = slowness.shape
    bins = rows_x * rows_y
    blocks = samples // LANES
    sources = got.shape[0] // ROWS
    items = CAP * sources
    edge = jax.ShapeDtypeStruct((rows_y, samples), F32)
    return pl.pallas_call(
        stack_kernel,
        in_specs=[VMEM] * 3,
        out_specs=[VMEM] * 3,
        out_shape=[jax.ShapeDtypeStruct((bins, samples), F32), edge, edge],
        scratch_shapes=[
            pltpu.VMEM((sources * ROWS, LANES), F32),
            pltpu.VMEM((blocks + 1, items, LANES), BF16),
            pltpu.VMEM((items, LANES), BF16),
            pltpu.VMEM((bins, items), BF16),
            pltpu.VMEM((bins, LANES), F32),
            pltpu.VMEM((3, items, LANES), F32),
            pltpu.VMEM((items, BAND * LANES), F32),
            pltpu.VMEM((items, BAND * LANES), F32),
            pltpu.VMEM((2 * items, LANES), BF16),
            pltpu.VMEM((2 * items, LANES), BF16),
        ],
        compiler_params=pltpu.CompilerParams(vmem_limit_bytes=40 << 20),
        name="stack",
    )(got, band_start.reshape(blocks, LANES), slowness)


def edges_kernel(stack_ref, low_ref, high_ref, first_ref, last_ref):
    height = low_ref.shape[0]
    width = stack_ref.shape[0] // height
    for y, ref in ((0, first_ref), (height - 1, last_ref)):
        ref[0:1, :] = low_ref[y : y + 1, :]
        for x in range(width):
            ref[x + 1 : x + 2, :] = stack_ref[x * height + y : x * height + y + 1, :]
        ref[width + 1 : width + 2, :] = high_ref[y : y + 1, :]


def edges(stacked, low, high):
    rows_y, samples = low.shape
    edge = jax.ShapeDtypeStruct((stacked.shape[0] // rows_y + 2, samples), F32)
    return pl.pallas_call(
        edges_kernel,
        in_specs=[VMEM] * 3,
        out_specs=[VMEM] * 2,
        out_shape=[edge, edge],
        compiler_params=pltpu.CompilerParams(vmem_limit_bytes=8 << 20),
        name="edges",
    )(stacked, low, high)


def inner_dip(dip, width, height):
    neighbour, bin_of = iota(dip.shape, 1), iota(dip.shape, 0)
    bin_x = lax.axis_index("xline") * width + bin_of // height + neighbour // 3 - 1
    bin_y = lax.axis_index("iline") * height + bin_of % height + neighbour % 3 - 1
    limit_x, limit_y = lax.axis_size("xline") * width, lax.axis_size("iline") * height
    inside = (bin_x >= 0) & (bin_x < limit_x) & (bin_y >= 0) & (bin_y < limit_y)
    return jnp.where(inside, dip, 2 * DIP + 1)


def steer(terms):
    shape = terms[0][0].shape
    samples = shape[1]
    time = iota(shape, 1)
    result = None
    for lag in range(-DIP, DIP + 1):
        part = None
        for rows, dip, factor in terms:
            value = jnp.where(dip == lag, factor, 0.0) * rows
            part = value if part is None else part + value
        if lag:
            part = pltpu.roll(part, (-lag) % samples, 1)
            part = jnp.where((time + lag >= 0) & (time + lag < samples), part, 0.0)
        result = part if result is None else result + part
    return result


def factor_of(n):
    return CENTER_WEIGHT if n == 4 else SIDE_WEIGHT


def smooth_kernel(stack_ref, low_ref, high_ref, dip_ref, out_ref, padded):
    height = low_ref.shape[0]
    bins, samples = stack_ref.shape
    width = bins // height
    pitch = height + 2
    zero = jnp.zeros((1, samples), F32)
    for x in range(width + 2):
        row = x * pitch
        padded[row : row + 1, :] = zero
        if x == 0:
            inner = low_ref[...]
        elif x == width + 1:
            inner = high_ref[...]
        else:
            inner = stack_ref[(x - 1) * height : x * height, :]
        padded[row + 1 : row + 1 + height, :] = inner
        padded[row + 1 + height : row + pitch, :] = zero
    dip = inner_dip(dip_ref[...], width, height)
    terms = []
    for n in range(9):
        dx, dy = n // 3, n % 3
        rows = [(dx + x) * pitch + dy for x in range(width)]
        near = jnp.concatenate([padded[r : r + height, :] for r in rows], axis=0)
        terms.append((near, dip[:, n : n + 1], factor_of(n)))
    out_ref[...] = steer(terms)


def border_kernel(part_ref, before_ref, after_ref, dip_ref, out_ref):
    width = before_ref.shape[0] - 2
    bins, samples = part_ref.shape
    height = bins // width
    dip = inner_dip(dip_ref[...], width, height)
    terms = []
    for dx in range(3):
        near = jnp.concatenate([before_ref[dx : dx + width, :], after_ref[dx : dx + width, :]], axis=0)
        shifts = [dip[x * height : x * height + 1, 3 * dx : 3 * dx + 1] for x in range(width)]
        shifts += [dip[(x + 1) * height - 1 : (x + 1) * height, 3 * dx + 2 : 3 * dx + 3] for x in range(width)]
        terms.append((near, jnp.concatenate(shifts, axis=0), SIDE_WEIGHT))
    border = steer(terms)
    for x in range(width):
        out_ref[x] = part_ref[x * height : (x + 1) * height, :]
        out_ref[x, 0:1, :] = part_ref[x * height : x * height + 1, :] + border[x : x + 1, :]
        last = (x + 1) * height - 1
        out_ref[x, height - 1 : height, :] = part_ref[last : last + 1, :] + border[width + x : width + x + 1, :]


def smooth(stacked, low, high, dip):
    rows_y, samples = low.shape
    bins = stacked.shape[0]
    rows_x = bins // rows_y
    return pl.pallas_call(
        smooth_kernel,
        in_specs=[VMEM] * 4,
        out_specs=VMEM,
        out_shape=jax.ShapeDtypeStruct((bins, samples), F32),
        scratch_shapes=[pltpu.VMEM(((rows_x + 2) * (rows_y + 2), samples), F32)],
        compiler_params=pltpu.CompilerParams(vmem_limit_bytes=8 << 20),
        name="smooth",
    )(stacked, low, high, dip)


def border(part, before, after, dip):
    bins, samples = part.shape
    rows_x = before.shape[0] - 2
    return pl.pallas_call(
        border_kernel,
        in_specs=[VMEM] * 4,
        out_specs=VMEM,
        out_shape=jax.ShapeDtypeStruct((rows_x, bins // rows_x, samples), F32),
        compiler_params=pltpu.CompilerParams(vmem_limit_bytes=8 << 20),
        name="border",
    )(part, before, after, dip)


def exchange(first, last, axis):
    size = lax.axis_size(axis)
    before = lax.ppermute(last, axis, [(i, (i + 1) % size) for i in range(size)])
    after = lax.ppermute(first, axis, [((i + 1) % size, i) for i in range(size)])
    return before, after


def body(traces, trace_offset, trace_owner, trace_cell, slowness, band_start, dip_shift):
    owners = lax.axis_size(AXES)
    rows_x, rows_y, samples = slowness.shape
    bins = rows_x * rows_y
    send = dispatch(traces, trace_owner, trace_cell, trace_offset, owners)
    send = send.reshape(owners, ROWS // 2, 2, LANES)
    got = lax.all_to_all(send, AXES, split_axis=0, concat_axis=0, tiled=True)
    stacked, first, last = stack(got.reshape(owners * ROWS, LANES), band_start, slowness)
    low, high = exchange(first, last, "xline")
    before, after = exchange(*edges(stacked, low, high), "iline")
    dip = dip_shift.reshape(9, bins).T
    return border(smooth(stacked, low, high, dip), before, after, dip)


def solution(mesh):
    return jax.shard_map(
        body,
        mesh=mesh,
        in_specs=(
            P(AXES, None),
            P(AXES),
            P(AXES),
            P(AXES),
            P("xline", "iline", None),
            P(),
            P(None, "xline", "iline"),
        ),
        out_specs=P("xline", "iline", None),
        check_vma=False,
    )
```

```python
import functools

import jax
import jax.numpy as jnp
from jax import lax
from jax.experimental import pallas as pl
from jax.experimental.pallas import tpu as pltpu
from jax.sharding import PartitionSpec as P

BAND = 8
DIP = 4
REACH = BAND - 1
LANES = 128
CAP = 5
ROWS = 62
REACHED = 144
DISPATCH_LIMIT = 24
STEP = 32
HALVES = (0.5, 1.5, 2.5, 3.5)
VMEM = pl.BlockSpec(memory_space=pltpu.VMEM)
HBM = pl.BlockSpec(memory_space=pltpu.HBM)

CENTER_WEIGHT = 0.5
SIDE_WEIGHT = 0.0625

AXES = ("xline", "iline")
F32 = jnp.float32
BF16 = jnp.bfloat16


def iota(shape, dim):
    return lax.broadcasted_iota(jnp.int32, shape, dim)


def in_line(value):
    return jnp.concatenate([value[i : i + 1, :] for i in range(value.shape[0])], axis=1)


def dispatch_kernel(owners, traces_hbm, owner_hbm, cell_hbm, offset_hbm, out_ref, traces_ref, owner_ref, cell_ref, offset_ref, stage, arrived):
    pairs = ((owner_hbm, owner_ref), (cell_hbm, cell_ref), (offset_hbm, offset_ref), (traces_hbm, traces_ref))
    copies = [pltpu.make_async_copy(there, here, arrived.at[i]) for i, (there, here) in enumerate(pairs)]
    for copy in copies:
        copy.start()
    rows, samples = traces_ref.shape
    blocks = samples // LANES
    for copy in copies[:3]:
        copy.wait()
    owner = in_line(owner_ref[...])
    hot = (iota((owners, rows), 0) == owner).astype(F32)
    earlier = (iota((rows, rows), 0) < iota((rows, rows), 1)).astype(F32).astype(BF16)
    counts = jnp.dot(hot.astype(BF16), earlier, preferred_element_type=F32)
    rank = jnp.sum(hot * counts, axis=0, keepdims=True)
    picks = [jnp.where(rank == float(k), hot, 0.0).astype(BF16) for k in range(CAP)]
    pick = jnp.concatenate(picks, axis=0)
    meta = jnp.zeros((owners, LANES), F32)
    line = iota((LANES, rows), 0)
    offset = in_line(offset_ref[...].astype(F32))
    cell = in_line(cell_ref[...] + 1).astype(F32)
    for k in range(CAP):
        source = jnp.where(line == 8 * k, offset, jnp.where(line == 8 * k + 1, cell, 0.0))
        meta = meta + lax.dot_general(
            picks[k], source.astype(BF16), (((1,), (1,)), ((), ())), preferred_element_type=F32
        )
    stage[pl.ds(CAP * blocks, owners, stride=ROWS), :] = meta
    for row in range(CAP * blocks + 1, ROWS):
        stage[pl.ds(row, owners, stride=ROWS), :] = jnp.zeros((owners, LANES), F32)
    copies[3].wait()
    wrapped = iota((rows, LANES), 1) < REACH

    def turned(block):
        return pltpu.roll(traces_ref[:, block * LANES : (block + 1) * LANES], REACH, 1)

    previous = turned(blocks - 1)
    for tile in range(0, blocks, 2):
        one, two = turned(tile), turned(tile + 1)
        moved = jnp.concatenate([jnp.where(wrapped, previous, one), jnp.where(wrapped, one, two)], axis=1)
        previous = two
        placed = jnp.dot(pick, moved, preferred_element_type=F32)
        for k in range(CAP):
            for half in range(2):
                stage[pl.ds(k * blocks + tile + half, owners, stride=ROWS), :] = placed[
                    k * owners : (k + 1) * owners, half * LANES : (half + 1) * LANES
                ]
    out_ref[...] = stage[...].astype(BF16)


def dispatch(traces, owner, cell, offset, owners):
    rows, samples = traces.shape
    given = [traces] + [v.reshape(rows // LANES, LANES) for v in (owner, cell, offset)]
    return pl.pallas_call(
        functools.partial(dispatch_kernel, owners),
        in_specs=[HBM] * 4,
        out_specs=VMEM,
        out_shape=jax.ShapeDtypeStruct((owners * ROWS, LANES), BF16),
        scratch_shapes=[
            pltpu.VMEM((rows, samples), BF16),
            pltpu.VMEM((rows // LANES, LANES), jnp.int32),
            pltpu.VMEM((rows // LANES, LANES), jnp.int32),
            pltpu.VMEM((rows // LANES, LANES), BF16),
            pltpu.VMEM((owners * ROWS, LANES), F32),
            pltpu.SemaphoreType.DMA((4,)),
        ],
        compiler_params=pltpu.CompilerParams(vmem_limit_bytes=DISPATCH_LIMIT << 20),
        name="dispatch",
    )(*(pltpu.with_memory_space_constraint(v, pltpu.HBM) for v in given))


def split3(value):
    high = value.astype(BF16)
    rest = value - high.astype(F32)
    middle = rest.astype(BF16)
    low = (rest - middle.astype(F32)).astype(BF16)
    return high, middle, low


def correct(lag, band):
    square = lag * lag
    num = odd = den = None
    for i, half in enumerate(HALVES):
        near = square + (1.0 + half * half)
        if half == 0.5:
            prod = near * near - square
        else:
            prod = (square + (2.0 - 2.0 * half * half)) * square + (1.0 + half * half) ** 2
        both = 1.0 / prod
        share = near * both
        part, tilt = band(2 * i) * share, band(2 * i + 1) * both
        num, odd, den = (part, tilt, share) if num is None else (num + part, odd + tilt, den + share)
    return (num + lag * odd) / den


def stack_kernel(got_ref, start_ref, slow_ref, out_ref, first_ref, last_ref, stage, window, scaled, member, fold, lags, pairs0, pairs1, moved0, moved1):
    blocks = start_ref.shape[0]
    bins = slow_ref.shape[0] * slow_ref.shape[1]
    sources = got_ref.shape[0] // ROWS
    items = CAP * sources
    stage[...] = got_ref[...].astype(F32)
    meta = stage[pl.ds(CAP * blocks, sources, stride=ROWS), :]
    across = meta.T
    lane = iota((sources, LANES), 1)
    total = jnp.zeros((bins, 1), F32)
    for k in range(CAP):
        here = slice(k * sources, (k + 1) * sources)
        offset = meta[:, 8 * k : 8 * k + 1]
        cell = meta[:, 8 * k + 1 : 8 * k + 2] - 1.0
        square = offset * offset
        high = square.astype(BF16).astype(F32)
        part = jnp.where(lane < 3 * bins, high, square - high)
        keep = ((lane % bins).astype(F32) == cell) & (lane < 6 * bins)
        ones = (lane >= 6 * bins) & (lane < 6 * bins + 3)
        scaled[here, :] = jnp.where(keep, part, jnp.where(ones, 1.0, 0.0)).astype(BF16)
        ones = (across[8 * k + 1 : 8 * k + 2, :] == (iota((bins, sources), 0) + 1).astype(F32)).astype(F32)
        total = total + jnp.sum(ones, axis=1, keepdims=True)
        member[:, here] = ones.astype(BF16)
    fold[...] = jnp.broadcast_to(jnp.maximum(total, 1.0), fold.shape)

    def gather(block):
        for k in range(CAP):
            rows = stage[pl.ds(k * blocks + block % blocks, sources, stride=ROWS), :]
            window[block, k * sources : (k + 1) * sources, :] = rows.astype(BF16)

    def lanes(block):
        return slice(block * LANES, (block + 1) * LANES)

    def shift(block):
        parts = list(split3(jnp.concatenate([slow_ref[x, :, lanes(block)] for x in range(slow_ref.shape[0])], axis=0)))
        ticks = iota((bins, LANES), 1) + block * LANES
        time = ticks.astype(F32)
        squares = split3(jnp.where(ticks == 0, 1e-30, time * time))
        line = iota((bins, LANES), 0)
        clock = jnp.zeros((bins, LANES), F32)
        for i, part in enumerate(squares):
            clock = jnp.where(line == i, part.astype(F32), clock)
        parts = [p.astype(F32) for p in parts + parts] + [clock, jnp.zeros((LANES - 7 * bins, LANES), F32)]
        total = jnp.dot(scaled[...], jnp.concatenate(parts, axis=0).astype(BF16), preferred_element_type=F32)
        lags[block % 3] = (start_ref[block : block + 1, :].astype(F32) + 3.5) - total * lax.rsqrt(total)

    def multiply(block, pairs):
        wide = jnp.concatenate([window[block], window[block + 1]], axis=1)
        first = start_ref[block : block + 1, :] + (REACH - block * LANES)
        place = (iota((REACHED, LANES), 0) - first).astype(F32) - 3.5
        back, apart = (-place).astype(BF16), jnp.abs(place).astype(BF16)
        none = jnp.zeros((REACHED, LANES), BF16)

        def pick(i):
            chosen = apart == jnp.asarray(HALVES[i], BF16)
            rows = jnp.concatenate([jnp.where(chosen, jnp.asarray(0.5, BF16), none), jnp.where(chosen, back, none)], axis=1)
            rows = jnp.concatenate([rows, jnp.zeros((2 * LANES - REACHED, 2 * LANES), BF16)], axis=0)
            pairs[:, 2 * i * LANES : 2 * (i + 1) * LANES] = jnp.dot(wide, rows, preferred_element_type=F32)

        return [functools.partial(pick, i) for i in range(BAND // 2)]

    def weigh(block, pairs, moved):
        def chunk(row):
            here = slice(row, row + STEP)
            lag = lags[block % 3, here, :]
            value = correct(lag, lambda i: pairs[here, i * LANES : (i + 1) * LANES])
            high = value.astype(BF16)
            moved[here, :] = high
            moved[items + row : items + row + STEP, :] = (value - high.astype(F32)).astype(BF16)

        return [functools.partial(chunk, row) for row in range(0, items, STEP)]

    def total_up(block, moved):
        sums = jnp.dot(member[...], moved[:items, :], preferred_element_type=F32) + jnp.dot(
            member[...], moved[items:, :], preferred_element_type=F32
        )
        mean = sums / fold[...]
        out_ref[:, lanes(block)] = mean
        first_ref[:, lanes(block)] = mean[: first_ref.shape[0], :]
        last_ref[:, lanes(block)] = mean[bins - last_ref.shape[0] :, :]

    def interleave(few, many):
        for i, work in enumerate(many):
            for j, other in enumerate(few):
                if j * len(many) // len(few) == i:
                    other()
            work()

    gather(0)
    gather(1)
    shift(0)
    shift(1)
    pairs, moved = (pairs0, pairs1), (moved0, moved1)
    for work in multiply(0, pairs0):
        work()
    for block in range(blocks):
        now, later = block % 2, (block + 1) % 2
        ahead = []
        if block + 1 < blocks:
            gather(block + 2)
            if block + 2 < blocks:
                shift(block + 2)
            ahead = multiply(block + 1, pairs[later])
        if block:
            total_up(block - 1, moved[later])
        interleave(ahead, weigh(block, pairs[now], moved[now]))
    total_up(blocks - 1, moved[(blocks - 1) % 2])


def stack(got, band_start, slowness):
    rows_x, rows_y, samples = slowness.shape
    bins = rows_x * rows_y
    blocks = samples // LANES
    sources = got.shape[0] // ROWS
    items = CAP * sources
    edge = jax.ShapeDtypeStruct((rows_y, samples), F32)
    return pl.pallas_call(
        stack_kernel,
        in_specs=[VMEM] * 3,
        out_specs=[VMEM] * 3,
        out_shape=[jax.ShapeDtypeStruct((bins, samples), F32), edge, edge],
        scratch_shapes=[
            pltpu.VMEM((sources * ROWS, LANES), F32),
            pltpu.VMEM((blocks + 1, items, LANES), BF16),
            pltpu.VMEM((items, LANES), BF16),
            pltpu.VMEM((bins, items), BF16),
            pltpu.VMEM((bins, LANES), F32),
            pltpu.VMEM((3, items, LANES), F32),
            pltpu.VMEM((items, BAND * LANES), F32),
            pltpu.VMEM((items, BAND * LANES), F32),
            pltpu.VMEM((2 * items, LANES), BF16),
            pltpu.VMEM((2 * items, LANES), BF16),
        ],
        compiler_params=pltpu.CompilerParams(vmem_limit_bytes=40 << 20),
        name="stack",
    )(got, band_start.reshape(blocks, LANES), slowness)


def edges_kernel(stack_ref, low_ref, high_ref, first_ref, last_ref):
    height = low_ref.shape[0]
    width = stack_ref.shape[0] // height
    for y, ref in ((0, first_ref), (height - 1, last_ref)):
        ref[0:1, :] = low_ref[y : y + 1, :]
        for x in range(width):
            ref[x + 1 : x + 2, :] = stack_ref[x * height + y : x * height + y + 1, :]
        ref[width + 1 : width + 2, :] = high_ref[y : y + 1, :]


def edges(stacked, low, high):
    rows_y, samples = low.shape
    edge = jax.ShapeDtypeStruct((stacked.shape[0] // rows_y + 2, samples), F32)
    return pl.pallas_call(
        edges_kernel,
        in_specs=[VMEM] * 3,
        out_specs=[VMEM] * 2,
        out_shape=[edge, edge],
        compiler_params=pltpu.CompilerParams(vmem_limit_bytes=8 << 20),
        name="edges",
    )(stacked, low, high)


def inner_dip(dip, width, height):
    neighbour, bin_of = iota(dip.shape, 1), iota(dip.shape, 0)
    bin_x = lax.axis_index("xline") * width + bin_of // height + neighbour // 3 - 1
    bin_y = lax.axis_index("iline") * height + bin_of % height + neighbour % 3 - 1
    limit_x, limit_y = lax.axis_size("xline") * width, lax.axis_size("iline") * height
    inside = (bin_x >= 0) & (bin_x < limit_x) & (bin_y >= 0) & (bin_y < limit_y)
    return jnp.where(inside, dip, 2 * DIP + 1)


def steer(terms):
    shape = terms[0][0].shape
    samples = shape[1]
    time = iota(shape, 1)
    result = None
    for lag in range(-DIP, DIP + 1):
        part = None
        for rows, dip, factor in terms:
            value = jnp.where(dip == lag, factor, 0.0) * rows
            part = value if part is None else part + value
        if lag:
            part = pltpu.roll(part, (-lag) % samples, 1)
            part = jnp.where((time + lag >= 0) & (time + lag < samples), part, 0.0)
        result = part if result is None else result + part
    return result


def factor_of(n):
    return CENTER_WEIGHT if n == 4 else SIDE_WEIGHT


def smooth_kernel(stack_ref, low_ref, high_ref, dip_ref, out_ref, padded):
    height = low_ref.shape[0]
    bins, samples = stack_ref.shape
    width = bins // height
    pitch = height + 2
    zero = jnp.zeros((1, samples), F32)
    for x in range(width + 2):
        row = x * pitch
        padded[row : row + 1, :] = zero
        if x == 0:
            inner = low_ref[...]
        elif x == width + 1:
            inner = high_ref[...]
        else:
            inner = stack_ref[(x - 1) * height : x * height, :]
        padded[row + 1 : row + 1 + height, :] = inner
        padded[row + 1 + height : row + pitch, :] = zero
    dip = inner_dip(dip_ref[...], width, height)
    terms = []
    for n in range(9):
        dx, dy = n // 3, n % 3
        rows = [(dx + x) * pitch + dy for x in range(width)]
        near = jnp.concatenate([padded[r : r + height, :] for r in rows], axis=0)
        terms.append((near, dip[:, n : n + 1], factor_of(n)))
    out_ref[...] = steer(terms)


def border_kernel(part_ref, before_ref, after_ref, dip_ref, out_ref):
    width = before_ref.shape[0] - 2
    bins, samples = part_ref.shape
    height = bins // width
    dip = inner_dip(dip_ref[...], width, height)
    terms = []
    for dx in range(3):
        near = jnp.concatenate([before_ref[dx : dx + width, :], after_ref[dx : dx + width, :]], axis=0)
        shifts = [dip[x * height : x * height + 1, 3 * dx : 3 * dx + 1] for x in range(width)]
        shifts += [dip[(x + 1) * height - 1 : (x + 1) * height, 3 * dx + 2 : 3 * dx + 3] for x in range(width)]
        terms.append((near, jnp.concatenate(shifts, axis=0), SIDE_WEIGHT))
    border = steer(terms)
    for x in range(width):
        out_ref[x] = part_ref[x * height : (x + 1) * height, :]
        out_ref[x, 0:1, :] = part_ref[x * height : x * height + 1, :] + border[x : x + 1, :]
        last = (x + 1) * height - 1
        out_ref[x, height - 1 : height, :] = part_ref[last : last + 1, :] + border[width + x : width + x + 1, :]


def smooth(stacked, low, high, dip):
    rows_y, samples = low.shape
    bins = stacked.shape[0]
    rows_x = bins // rows_y
    return pl.pallas_call(
        smooth_kernel,
        in_specs=[VMEM] * 4,
        out_specs=VMEM,
        out_shape=jax.ShapeDtypeStruct((bins, samples), F32),
        scratch_shapes=[pltpu.VMEM(((rows_x + 2) * (rows_y + 2), samples), F32)],
        compiler_params=pltpu.CompilerParams(vmem_limit_bytes=8 << 20),
        name="smooth",
    )(stacked, low, high, dip)


def border(part, before, after, dip):
    bins, samples = part.shape
    rows_x = before.shape[0] - 2
    return pl.pallas_call(
        border_kernel,
        in_specs=[VMEM] * 4,
        out_specs=VMEM,
        out_shape=jax.ShapeDtypeStruct((rows_x, bins // rows_x, samples), F32),
        compiler_params=pltpu.CompilerParams(vmem_limit_bytes=8 << 20),
        name="border",
    )(part, before, after, dip)


def exchange(first, last, axis):
    size = lax.axis_size(axis)
    before = lax.ppermute(last, axis, [(i, (i + 1) % size) for i in range(size)])
    after = lax.ppermute(first, axis, [((i + 1) % size, i) for i in range(size)])
    return before, after


def body(traces, trace_offset, trace_owner, trace_cell, slowness, band_start, dip_shift):
    owners = lax.axis_size(AXES)
    rows_x, rows_y, samples = slowness.shape
    bins = rows_x * rows_y
    send = dispatch(traces, trace_owner, trace_cell, trace_offset, owners)
    send = send.reshape(owners, ROWS // 2, 2, LANES)
    got = lax.all_to_all(send, AXES, split_axis=0, concat_axis=0, tiled=True)
    stacked, first, last = stack(got.reshape(owners * ROWS, LANES), band_start, slowness)
    low, high = exchange(first, last, "xline")
    before, after = exchange(*edges(stacked, low, high), "iline")
    dip = dip_shift.reshape(9, bins).T
    return border(smooth(stacked, low, high, dip), before, after, dip)


def solution(mesh):
    return jax.shard_map(
        body,
        mesh=mesh,
        in_specs=(
            P(AXES, None),
            P(AXES),
            P(AXES),
            P(AXES),
            P("xline", "iline", None),
            P(),
            P(None, "xline", "iline"),
        ),
        out_specs=P("xline", "iline", None),
        check_vma=False,
    )
```

```python
import functools

import jax
import jax.numpy as jnp
from jax import lax
from jax.experimental import pallas as pl
from jax.experimental.pallas import tpu as pltpu
from jax.sharding import PartitionSpec as P

BAND = 8
DIP = 4
REACH = BAND - 1
LANES = 128
CAP = 5
ROWS = 62
REACHED = 144
DISPATCH_LIMIT = 24
STEP = 32
HALVES = (0.5, 1.5, 2.5, 3.5)
VMEM = pl.BlockSpec(memory_space=pltpu.VMEM)
HBM = pl.BlockSpec(memory_space=pltpu.HBM)

CENTER_WEIGHT = 0.5
SIDE_WEIGHT = 0.0625

AXES = ("xline", "iline")
F32 = jnp.float32
BF16 = jnp.bfloat16


def iota(shape, dim):
    return lax.broadcasted_iota(jnp.int32, shape, dim)


def in_line(value):
    return jnp.concatenate([value[i : i + 1, :] for i in range(value.shape[0])], axis=1)


def dispatch_kernel(owners, traces_hbm, owner_hbm, cell_hbm, offset_hbm, out_ref, traces_ref, owner_ref, cell_ref, offset_ref, stage, arrived):
    pairs = ((owner_hbm, owner_ref), (cell_hbm, cell_ref), (offset_hbm, offset_ref), (traces_hbm, traces_ref))
    copies = [pltpu.make_async_copy(there, here, arrived.at[i]) for i, (there, here) in enumerate(pairs)]
    for copy in copies:
        copy.start()
    rows, samples = traces_ref.shape
    blocks = samples // LANES
    for copy in copies[:3]:
        copy.wait()
    owner = in_line(owner_ref[...])
    hot = (iota((owners, rows), 0) == owner).astype(F32)
    earlier = (iota((rows, rows), 0) < iota((rows, rows), 1)).astype(F32).astype(BF16)
    counts = jnp.dot(hot.astype(BF16), earlier, preferred_element_type=F32)
    rank = jnp.sum(hot * counts, axis=0, keepdims=True)
    picks = [jnp.where(rank == float(k), hot, 0.0).astype(BF16) for k in range(CAP)]
    pick = jnp.concatenate(picks, axis=0)
    meta = jnp.zeros((owners, LANES), F32)
    line = iota((LANES, rows), 0)
    offset = in_line(offset_ref[...].astype(F32))
    cell = in_line(cell_ref[...] + 1).astype(F32)
    for k in range(CAP):
        source = jnp.where(line == 8 * k, offset, jnp.where(line == 8 * k + 1, cell, 0.0))
        meta = meta + lax.dot_general(
            picks[k], source.astype(BF16), (((1,), (1,)), ((), ())), preferred_element_type=F32
        )
    stage[pl.ds(CAP * blocks, owners, stride=ROWS), :] = meta
    for row in range(CAP * blocks + 1, ROWS):
        stage[pl.ds(row, owners, stride=ROWS), :] = jnp.zeros((owners, LANES), F32)
    copies[3].wait()
    wrapped = iota((rows, LANES), 1) < REACH

    def turned(block):
        return pltpu.roll(traces_ref[:, block * LANES : (block + 1) * LANES], REACH, 1)

    previous = turned(blocks - 1)
    for tile in range(0, blocks, 2):
        one, two = turned(tile), turned(tile + 1)
        moved = jnp.concatenate([jnp.where(wrapped, previous, one), jnp.where(wrapped, one, two)], axis=1)
        previous = two
        placed = jnp.dot(pick, moved, preferred_element_type=F32)
        for k in range(CAP):
            for half in range(2):
                stage[pl.ds(k * blocks + tile + half, owners, stride=ROWS), :] = placed[
                    k * owners : (k + 1) * owners, half * LANES : (half + 1) * LANES
                ]
    out_ref[...] = stage[...].astype(BF16)


def dispatch(traces, owner, cell, offset, owners):
    rows, samples = traces.shape
    given = [traces] + [v.reshape(rows // LANES, LANES) for v in (owner, cell, offset)]
    return pl.pallas_call(
        functools.partial(dispatch_kernel, owners),
        in_specs=[HBM] * 4,
        out_specs=VMEM,
        out_shape=jax.ShapeDtypeStruct((owners * ROWS, LANES), BF16),
        scratch_shapes=[
            pltpu.VMEM((rows, samples), BF16),
            pltpu.VMEM((rows // LANES, LANES), jnp.int32),
            pltpu.VMEM((rows // LANES, LANES), jnp.int32),
            pltpu.VMEM((rows // LANES, LANES), BF16),
            pltpu.VMEM((owners * ROWS, LANES), F32),
            pltpu.SemaphoreType.DMA((4,)),
        ],
        compiler_params=pltpu.CompilerParams(vmem_limit_bytes=DISPATCH_LIMIT << 20),
        name="dispatch",
    )(*(pltpu.with_memory_space_constraint(v, pltpu.HBM) for v in given))


def split3(value):
    high = value.astype(BF16)
    rest = value - high.astype(F32)
    middle = rest.astype(BF16)
    low = (rest - middle.astype(F32)).astype(BF16)
    return high, middle, low


def correct(lag, band):
    square = lag * lag
    num = odd = den = None
    for i, half in enumerate(HALVES):
        near = square + (1.0 + half * half)
        if half == 0.5:
            prod = near * near - square
        else:
            prod = (square + (2.0 - 2.0 * half * half)) * square + (1.0 + half * half) ** 2
        both = 1.0 / prod
        share = near * both
        part, tilt = band(2 * i) * share, band(2 * i + 1) * both
        num, odd, den = (part, tilt, share) if num is None else (num + part, odd + tilt, den + share)
    return (num + lag * odd) / den


def stack_kernel(got_ref, start_ref, slow_ref, out_ref, first_ref, last_ref, stage, window, scaled, member, fold, lags, pairs0, pairs1, moved0, moved1):
    blocks = start_ref.shape[0]
    bins = slow_ref.shape[0] * slow_ref.shape[1]
    sources = got_ref.shape[0] // ROWS
    items = CAP * sources
    stage[...] = got_ref[...].astype(F32)
    meta = stage[pl.ds(CAP * blocks, sources, stride=ROWS), :]
    across = meta.T
    lane = iota((sources, LANES), 1)
    total = jnp.zeros((bins, 1), F32)
    for k in range(CAP):
        here = slice(k * sources, (k + 1) * sources)
        offset = meta[:, 8 * k : 8 * k + 1]
        cell = meta[:, 8 * k + 1 : 8 * k + 2] - 1.0
        square = offset * offset
        high = square.astype(BF16).astype(F32)
        part = jnp.where(lane < 3 * bins, high, square - high)
        keep = ((lane % bins).astype(F32) == cell) & (lane < 6 * bins)
        ones = (lane >= 6 * bins) & (lane < 6 * bins + 3)
        scaled[here, :] = jnp.where(keep, part, jnp.where(ones, 1.0, 0.0)).astype(BF16)
        ones = (across[8 * k + 1 : 8 * k + 2, :] == (iota((bins, sources), 0) + 1).astype(F32)).astype(F32)
        total = total + jnp.sum(ones, axis=1, keepdims=True)
        member[:, here] = ones.astype(BF16)
    fold[...] = jnp.broadcast_to(jnp.maximum(total, 1.0), fold.shape)

    def gather(block):
        for k in range(CAP):
            rows = stage[pl.ds(k * blocks + block % blocks, sources, stride=ROWS), :]
            window[block, k * sources : (k + 1) * sources, :] = rows.astype(BF16)

    def lanes(block):
        return slice(block * LANES, (block + 1) * LANES)

    def shift(block):
        parts = list(split3(jnp.concatenate([slow_ref[x, :, lanes(block)] for x in range(slow_ref.shape[0])], axis=0)))
        ticks = iota((bins, LANES), 1) + block * LANES
        time = ticks.astype(F32)
        squares = split3(jnp.where(ticks == 0, 1e-30, time * time))
        line = iota((bins, LANES), 0)
        clock = jnp.zeros((bins, LANES), F32)
        for i, part in enumerate(squares):
            clock = jnp.where(line == i, part.astype(F32), clock)
        parts = [p.astype(F32) for p in parts + parts] + [clock, jnp.zeros((LANES - 7 * bins, LANES), F32)]
        total = jnp.dot(scaled[...], jnp.concatenate(parts, axis=0).astype(BF16), preferred_element_type=F32)
        lags[block % 3] = (start_ref[block : block + 1, :].astype(F32) + 3.5) - total * lax.rsqrt(total)

    def multiply(block, pairs):
        wide = jnp.concatenate([window[block], window[block + 1]], axis=1)
        first = start_ref[block : block + 1, :] + (REACH - block * LANES)
        place = (iota((REACHED, LANES), 0) - first).astype(F32) - 3.5
        back, apart = (-place).astype(BF16), jnp.abs(place).astype(BF16)
        none = jnp.zeros((REACHED, LANES), BF16)

        def pick(i):
            chosen = apart == jnp.asarray(HALVES[i], BF16)
            rows = jnp.concatenate([jnp.where(chosen, jnp.asarray(0.5, BF16), none), jnp.where(chosen, back, none)], axis=1)
            rows = jnp.concatenate([rows, jnp.zeros((2 * LANES - REACHED, 2 * LANES), BF16)], axis=0)
            pairs[:, 2 * i * LANES : 2 * (i + 1) * LANES] = jnp.dot(wide, rows, preferred_element_type=F32)

        return [functools.partial(pick, i) for i in range(BAND // 2)]

    def weigh(block, pairs, moved):
        def chunk(row):
            here = slice(row, row + STEP)
            lag = lags[block % 3, here, :]
            value = correct(lag, lambda i: pairs[here, i * LANES : (i + 1) * LANES])
            high = value.astype(BF16)
            moved[here, :] = high
            moved[items + row : items + row + STEP, :] = (value - high.astype(F32)).astype(BF16)

        return [functools.partial(chunk, row) for row in range(0, items, STEP)]

    def total_up(block, moved):
        sums = jnp.dot(member[...], moved[:items, :], preferred_element_type=F32) + jnp.dot(
            member[...], moved[items:, :], preferred_element_type=F32
        )
        out_ref[:, lanes(block)] = sums / fold[...]

    def interleave(few, many):
        for i, work in enumerate(many):
            for j, other in enumerate(few):
                if j * len(many) // len(few) == i:
                    other()
            work()

    gather(0)
    gather(1)
    shift(0)
    shift(1)
    pairs, moved = (pairs0, pairs1), (moved0, moved1)
    for work in multiply(0, pairs0):
        work()
    for block in range(blocks):
        now, later = block % 2, (block + 1) % 2
        ahead = []
        if block + 1 < blocks:
            gather(block + 2)
            if block + 2 < blocks:
                shift(block + 2)
            ahead = multiply(block + 1, pairs[later])
        if block:
            total_up(block - 1, moved[later])
        interleave(ahead, weigh(block, pairs[now], moved[now]))
    total_up(blocks - 1, moved[(blocks - 1) % 2])
    first_ref[...] = out_ref[: first_ref.shape[0], :]
    last_ref[...] = out_ref[bins - last_ref.shape[0] :, :]


def stack(got, band_start, slowness):
    rows_x, rows_y, samples = slowness.shape
    bins = rows_x * rows_y
    blocks = samples // LANES
    sources = got.shape[0] // ROWS
    items = CAP * sources
    edge = jax.ShapeDtypeStruct((rows_y, samples), F32)
    return pl.pallas_call(
        stack_kernel,
        in_specs=[VMEM] * 3,
        out_specs=[VMEM] * 3,
        out_shape=[jax.ShapeDtypeStruct((bins, samples), F32), edge, edge],
        scratch_shapes=[
            pltpu.VMEM((sources * ROWS, LANES), F32),
            pltpu.VMEM((blocks + 1, items, LANES), BF16),
            pltpu.VMEM((items, LANES), BF16),
            pltpu.VMEM((bins, items), BF16),
            pltpu.VMEM((bins, LANES), F32),
            pltpu.VMEM((3, items, LANES), F32),
            pltpu.VMEM((items, BAND * LANES), F32),
            pltpu.VMEM((items, BAND * LANES), F32),
            pltpu.VMEM((2 * items, LANES), BF16),
            pltpu.VMEM((2 * items, LANES), BF16),
        ],
        compiler_params=pltpu.CompilerParams(vmem_limit_bytes=40 << 20),
        name="stack",
    )(got, band_start.reshape(blocks, LANES), slowness)


def edges_kernel(stack_ref, low_ref, high_ref, first_ref, last_ref):
    height = low_ref.shape[0]
    width = stack_ref.shape[0] // height
    for y, ref in ((0, first_ref), (height - 1, last_ref)):
        ref[0:1, :] = low_ref[y : y + 1, :]
        for x in range(width):
            ref[x + 1 : x + 2, :] = stack_ref[x * height + y : x * height + y + 1, :]
        ref[width + 1 : width + 2, :] = high_ref[y : y + 1, :]


def edges(stacked, low, high):
    rows_y, samples = low.shape
    edge = jax.ShapeDtypeStruct((stacked.shape[0] // rows_y + 2, samples), F32)
    return pl.pallas_call(
        edges_kernel,
        in_specs=[VMEM] * 3,
        out_specs=[VMEM] * 2,
        out_shape=[edge, edge],
        compiler_params=pltpu.CompilerParams(vmem_limit_bytes=8 << 20),
        name="edges",
    )(stacked, low, high)


def inner_dip(dip, width, height):
    neighbour, bin_of = iota(dip.shape, 1), iota(dip.shape, 0)
    bin_x = lax.axis_index("xline") * width + bin_of // height + neighbour // 3 - 1
    bin_y = lax.axis_index("iline") * height + bin_of % height + neighbour % 3 - 1
    limit_x, limit_y = lax.axis_size("xline") * width, lax.axis_size("iline") * height
    inside = (bin_x >= 0) & (bin_x < limit_x) & (bin_y >= 0) & (bin_y < limit_y)
    return jnp.where(inside, dip, 2 * DIP + 1)


def steer(terms):
    shape = terms[0][0].shape
    samples = shape[1]
    time = iota(shape, 1)
    result = None
    for lag in range(-DIP, DIP + 1):
        part = None
        for rows, dip, factor in terms:
            value = jnp.where(dip == lag, factor, 0.0) * rows
            part = value if part is None else part + value
        if lag:
            part = pltpu.roll(part, (-lag) % samples, 1)
            part = jnp.where((time + lag >= 0) & (time + lag < samples), part, 0.0)
        result = part if result is None else result + part
    return result


def factor_of(n):
    return CENTER_WEIGHT if n == 4 else SIDE_WEIGHT


def smooth_kernel(stack_ref, low_ref, high_ref, dip_ref, out_ref, padded):
    height = low_ref.shape[0]
    bins, samples = stack_ref.shape
    width = bins // height
    pitch = height + 2
    zero = jnp.zeros((1, samples), F32)
    for x in range(width + 2):
        row = x * pitch
        padded[row : row + 1, :] = zero
        if x == 0:
            inner = low_ref[...]
        elif x == width + 1:
            inner = high_ref[...]
        else:
            inner = stack_ref[(x - 1) * height : x * height, :]
        padded[row + 1 : row + 1 + height, :] = inner
        padded[row + 1 + height : row + pitch, :] = zero
    dip = inner_dip(dip_ref[...], width, height)
    terms = []
    for n in range(9):
        dx, dy = n // 3, n % 3
        rows = [(dx + x) * pitch + dy for x in range(width)]
        near = jnp.concatenate([padded[r : r + height, :] for r in rows], axis=0)
        terms.append((near, dip[:, n : n + 1], factor_of(n)))
    out_ref[...] = steer(terms)


def border_kernel(part_ref, before_ref, after_ref, dip_ref, out_ref):
    width = before_ref.shape[0] - 2
    bins, samples = part_ref.shape
    height = bins // width
    dip = inner_dip(dip_ref[...], width, height)
    terms = []
    for dx in range(3):
        near = jnp.concatenate([before_ref[dx : dx + width, :], after_ref[dx : dx + width, :]], axis=0)
        shifts = [dip[x * height : x * height + 1, 3 * dx : 3 * dx + 1] for x in range(width)]
        shifts += [dip[(x + 1) * height - 1 : (x + 1) * height, 3 * dx + 2 : 3 * dx + 3] for x in range(width)]
        terms.append((near, jnp.concatenate(shifts, axis=0), SIDE_WEIGHT))
    border = steer(terms)
    for x in range(width):
        out_ref[x] = part_ref[x * height : (x + 1) * height, :]
        out_ref[x, 0:1, :] = part_ref[x * height : x * height + 1, :] + border[x : x + 1, :]
        last = (x + 1) * height - 1
        out_ref[x, height - 1 : height, :] = part_ref[last : last + 1, :] + border[width + x : width + x + 1, :]


def smooth(stacked, low, high, dip):
    rows_y, samples = low.shape
    bins = stacked.shape[0]
    rows_x = bins // rows_y
    return pl.pallas_call(
        smooth_kernel,
        in_specs=[VMEM] * 4,
        out_specs=VMEM,
        out_shape=jax.ShapeDtypeStruct((bins, samples), F32),
        scratch_shapes=[pltpu.VMEM(((rows_x + 2) * (rows_y + 2), samples), F32)],
        compiler_params=pltpu.CompilerParams(vmem_limit_bytes=8 << 20),
        name="smooth",
    )(stacked, low, high, dip)


def border(part, before, after, dip):
    bins, samples = part.shape
    rows_x = before.shape[0] - 2
    return pl.pallas_call(
        border_kernel,
        in_specs=[VMEM] * 4,
        out_specs=VMEM,
        out_shape=jax.ShapeDtypeStruct((rows_x, bins // rows_x, samples), F32),
        compiler_params=pltpu.CompilerParams(vmem_limit_bytes=8 << 20),
        name="border",
    )(part, before, after, dip)


def exchange(first, last, axis):
    size = lax.axis_size(axis)
    before = lax.ppermute(last, axis, [(i, (i + 1) % size) for i in range(size)])
    after = lax.ppermute(first, axis, [((i + 1) % size, i) for i in range(size)])
    return before, after


def body(traces, trace_offset, trace_owner, trace_cell, slowness, band_start, dip_shift):
    owners = lax.axis_size(AXES)
    rows_x, rows_y, samples = slowness.shape
    bins = rows_x * rows_y
    send = dispatch(traces, trace_owner, trace_cell, trace_offset, owners)
    send = send.reshape(owners, ROWS // 2, 2, LANES)
    got = lax.all_to_all(send, AXES, split_axis=0, concat_axis=0, tiled=True)
    stacked, first, last = stack(got.reshape(owners * ROWS, LANES), band_start, slowness)
    low, high = exchange(first, last, "xline")
    before, after = exchange(*edges(stacked, low, high), "iline")
    dip = dip_shift.reshape(9, bins).T
    return border(smooth(stacked, low, high, dip), before, after, dip)


def solution(mesh):
    return jax.shard_map(
        body,
        mesh=mesh,
        in_specs=(
            P(AXES, None),
            P(AXES),
            P(AXES),
            P(AXES),
            P("xline", "iline", None),
            P(),
            P(None, "xline", "iline"),
        ),
        out_specs=P("xline", "iline", None),
        check_vma=False,
    )
```
